32 devices in a mesh: grp: 2 (over y), tile: 16 (over z, x, core).
Axes of the slice: x: 2, y: 2, z: 4, core: 2. Of those that a mesh axis runs over, the one named last changes fastest.
Arguments:
- rhs: float32 [256, 28672], P('grp', 'tile'), parts along dimension 0, may hold values from -4.5 to 4.5
- mass_diag: float32 [28672], P('tile'), may hold values from 0.1 to 2
- edge_heads: int32 [114688], P('tile'), may hold values from 128 to 1919
- edge_tails: int32 [114688], P('tile'), may hold values from 0 to 2047
- edge_weight: float32 [114688], P('tile'), may hold values from 0.5 to 2
- local_inverse: bfloat16 [32768, 2048], P('tile'), may hold values from -0.5 to 1
- coarse_vec: float32 [28672], P('tile'), may hold values from 0.25 to 1.75
- coarse_inv: float32 [16, 16], replicated, may hold values from -0.000558035714 to 0.002232143
Outputs:
- solution: float32 [256, 28672], P('grp', 'tile'), parts along dimension 0
- residual: float32 [256, 28672], P('grp', 'tile'), parts along dimension 0
The draws below stay inside these ranges and needn't reach their ends.
There are 2 independent parts, one for each index of `grp`. The reference program is written for one: setup_inputs(seed, part) draws one part's arguments, and reference() takes and returns one part's arrays. A program takes and returns all parts, laid end to end along the dimension named above; an argument that names none is the same for every part. Nothing has to cross between parts.
All inputs are finite; a program needn't handle non-finite values.
Results may differ from the reference program's by a relative error of at most 0.015.
Values may be sent and summed in bfloat16 or wider, within the bound.
No kernel may reach another device: no remote copies, remote signals or barrier semaphores. Data moves between devices by JAX's collectives and lax.ppermute only.
A program may use at most 128 MiB of HBM per device.

```python
import math
import jax
import jax.numpy as jnp
from jax import lax

SUB = 2048
STRIP = 128
RHS = 128
ITERS = 2
OWN = 1792
EDGE_DEV = 7168
TILES = 16
NODES = 28672
EDGES = 114688


def draw_rhs(key, part):
    first, second = jax.random.split(jax.random.fold_in(key, 11))
    noise = jax.random.truncated_normal(first, -3.0, 3.0, (RHS, NODES), jnp.float32)
    offset = jax.random.uniform(second, (RHS, TILES), jnp.float32, -1.5, 1.5)
    return (noise.reshape(RHS, TILES, OWN) + offset[:, :, None]).reshape(RHS, NODES)


def draw_local_inverse(key, part):
    first = jax.random.fold_in(key, 23)
    raw = jax.random.truncated_normal(first, -4.0, 4.0, (TILES, SUB, SUB), jnp.float32)
    raw = (raw + jnp.swapaxes(raw, 1, 2)) / jnp.sqrt(jnp.float32(2.0))
    raw = raw / jnp.sqrt(jnp.float32(SUB))
    diag_idx = jnp.arange(SUB)
    raw = raw.at[:, diag_idx, diag_idx].add(3.0)
    return (0.25 * raw).reshape(TILES * SUB, SUB).astype(jnp.bfloat16)


def draw_coarse_inv(key, part):
    first, second = jax.random.split(jax.random.fold_in(key, 37))
    diag = jnp.exp(jax.random.uniform(first, (TILES,), jnp.float32, 0.0, jnp.log(3.0)))
    off = jax.random.truncated_normal(second, -3.0, 3.0, (TILES, TILES), jnp.float32)
    off = (off + off.T) / jnp.sqrt(jnp.float32(2.0))
    mat = jnp.diag(diag) + off * (0.4 / jnp.sqrt(jnp.float32(TILES)))
    return mat / OWN


def set_ends(drawn, key, least, top_value):
    place = [jax.random.randint(jax.random.fold_in(key, axis), (), 0, length) for axis, length in enumerate(drawn.shape)]
    widest = drawn.shape.index(max(drawn.shape))
    beside = place[:widest] + [(place[widest] + 1) % drawn.shape[widest]] + place[widest + 1:]
    return drawn.at[tuple(place)].set(least).at[tuple(beside)].set(top_value)


def levels(own_key, extent, cuts, smallest, largest):
    loudness = 1.0
    for dim, blocks in cuts:
        heights = jax.random.uniform(jax.random.fold_in(jax.random.fold_in(own_key, 6), dim), (blocks,), jnp.float32, smallest / len(cuts), largest / len(cuts))
        loudness = loudness * jnp.repeat(jnp.exp(heights), extent[dim] // blocks).reshape((-1,) + (1,) * (len(extent) - 1 - dim))
    return loudness


def setup_inputs(seed: int = 0, part: int = 0) -> dict:
    keys = jax.random.split(jax.random.key(seed), 9)
    part_splits = jax.random.split(jax.random.fold_in(keys[8], part), 9)
    rhs = draw_rhs(jax.random.fold_in(jax.random.fold_in(keys[8], part), 71), part)
    mass_diag = jnp.clip(jnp.exp(math.log(2.0) - 2.9957323 * jax.random.uniform(keys[1], (NODES,), jnp.float32) ** levels(keys[1], (NODES,), ((0, 16),), -0.2, 0.2)), 0.1, 2.0)
    edge_heads = set_ends(jax.random.randint(keys[2], (EDGES,), STRIP, STRIP + OWN), jax.random.fold_in(keys[2], 1), STRIP, (STRIP + OWN) - 1).astype(jnp.int32)
    edge_tails = set_ends(jax.random.randint(keys[3], (EDGES,), 0, SUB), jax.random.fold_in(keys[3], 1), 0, SUB - 1).astype(jnp.int32)
    edge_weight = jnp.clip(jnp.exp(math.log(2.0) - 1.3862944 * jax.random.uniform(keys[4], (EDGES,), jnp.float32) ** levels(keys[4], (EDGES,), ((0, 16),), -0.2, 0.2)), 0.5, 2.0)
    local_inverse = draw_local_inverse(jax.random.fold_in(keys[8], 71), part)
    coarse_vec = jnp.clip(1.0 + 0.15 * jax.random.normal(keys[6], (NODES,), jnp.float32), 0.25, 1.75)
    coarse_inv = draw_coarse_inv(jax.random.fold_in(keys[8], 71), part)
    return {"rhs": rhs, "mass_diag": mass_diag, "edge_heads": edge_heads, "edge_tails": edge_tails, "edge_weight": edge_weight, "local_inverse": local_inverse, "coarse_vec": coarse_vec, "coarse_inv": coarse_inv}


def operate(v, mass_diag, edge_heads, edge_tails, edge_weight):
    base = (jnp.arange(EDGES, dtype=jnp.int32) // EDGE_DEV) * OWN
    head = (base + edge_heads).astype(jnp.int32)
    tail = (base + edge_tails).astype(jnp.int32)

    def one_row(row):
        padded = jnp.pad(row, (STRIP, STRIP))
        diff = edge_weight * (padded[head] - padded[tail])
        acc = jnp.zeros_like(padded).at[head].add(diff).at[tail].add(-diff)
        return mass_diag * row + acc[STRIP:STRIP + NODES]

    return lax.map(one_row, v)


def precondition(resid, local_inverse, coarse_vec, coarse_inv):
    padded = jnp.pad(resid, ((0, 0), (STRIP, STRIP))).astype(jnp.bfloat16)

    def add_block(acc, tile):
        start = (tile * OWN).astype(jnp.int32)
        piece = lax.dynamic_slice(padded, (jnp.int32(0), start), (RHS, SUB))
        block = lax.dynamic_slice(local_inverse, ((tile * SUB).astype(jnp.int32), jnp.int32(0)), (SUB, SUB))
        local = jnp.dot(piece, block, preferred_element_type=jnp.float32)
        old = lax.dynamic_slice(acc, (jnp.int32(0), start), (RHS, SUB))
        return lax.dynamic_update_slice(acc, old + local, (jnp.int32(0), start)), None

    start_acc = jnp.zeros((RHS, NODES + 2 * STRIP), jnp.float32)
    acc, _ = lax.scan(add_block, start_acc, jnp.arange(TILES, dtype=jnp.int32))
    schwarz = acc[:, STRIP:STRIP + NODES]
    shaped = coarse_vec.reshape(TILES, OWN)
    restricted = jnp.sum(resid.reshape(RHS, TILES, OWN) * shaped, axis=2)
    coarse = jnp.dot(restricted, coarse_inv, precision=lax.Precision.HIGHEST)
    return schwarz + (coarse[:, :, None] * shaped).reshape(RHS, NODES)


def reference(rhs, mass_diag, edge_heads, edge_tails, edge_weight, local_inverse, coarse_vec, coarse_inv):
    solution = jnp.zeros_like(rhs)
    resid = rhs
    zvec = precondition(resid, local_inverse, coarse_vec, coarse_inv)
    direction = zvec
    rz_now = jnp.sum(resid * zvec, axis=1)
    for step in range(ITERS):
        image = operate(direction, mass_diag, edge_heads, edge_tails, edge_weight)
        alpha = rz_now / jnp.sum(direction * image, axis=1)
        solution = solution + alpha[:, None] * direction
        resid = resid - alpha[:, None] * image
        if step + 1 < ITERS:
            zvec = precondition(resid, local_inverse, coarse_vec, coarse_inv)
            rz_next = jnp.sum(resid * zvec, axis=1)
            direction = zvec + (rz_next / rz_now)[:, None] * direction
            rz_now = rz_next
    return solution, resid
```

```python
import functools

import jax
import jax.numpy as jnp
from jax import lax
from jax.experimental import pallas as pl
from jax.experimental.pallas import tpu as pltpu
from jax.sharding import PartitionSpec as P

STRIP = 128
LANES = 128
GROUP = 16
F32 = jnp.float32
BF16 = jnp.bfloat16
NN = (((1,), (0,)), ((), ()))
NT = (((1,), (1,)), ((), ()))
TN = (((0,), (0,)), ((), ()))
HIGHEST = lax.Precision.HIGHEST


def up(value, unit):
    return -(-value // unit) * unit


def iota(shape, dim):
    return lax.broadcasted_iota(jnp.int32, shape, dim)


def place():
    me = lax.axis_index("tile").astype(jnp.int32)
    return me, lax.rem(me, jnp.int32(2)) == 0


def ends(n):
    me, _ = place()
    return (
        jnp.where(me > 0, 1.0, 0.0).astype(F32),
        jnp.where(me < n - 1, 1.0, 0.0).astype(F32),
    )


def put_sides(even_ref, odd_ref, left, right):
    _, even = place()

    @pl.when(even)
    def _():
        even_ref[...] = right
        odd_ref[...] = left

    @pl.when(jnp.logical_not(even))
    def _():
        even_ref[...] = left
        odd_ref[...] = right


def take_sides(even_got, odd_got):
    _, even = place()
    flag = jnp.where(even, 1.0, 0.0).astype(F32)
    a, b = even_got.astype(F32), odd_got.astype(F32)
    return jnp.where(flag > 0, b, a), jnp.where(flag > 0, a, b)


def widen(own_ref, got_left, got_right, n, inner):
    first, last = ends(n)
    w = STRIP
    sub = own_ref.shape[1]
    parts = [
        (own_ref[:, 0:w] + got_left[:, 0:w]) * first,
        own_ref[:, w : 2 * w] + got_left[:, w:],
        own_ref[:, 2 * w : sub - 2 * w],
        own_ref[:, sub - 2 * w : sub - w] + got_right[:, 0:w],
        (own_ref[:, sub - w :] + got_right[:, w:]) * last,
    ]
    return parts


def rows_of(columns, count):
    rhs = columns[0][1].shape[0]
    wide = up(count, LANES)
    lane = iota((rhs, wide), 1)
    total = jnp.zeros((rhs, wide), F32)
    for slot, column in columns:
        total = total + jnp.where(lane == slot, jnp.broadcast_to(column, (rhs, wide)), 0.0)
    return jnp.transpose(total)


def rowsum(x):
    return jnp.sum(x, axis=1, keepdims=True)


def begin_kernel(n, rhs_ref, cvec_ref, mass_ref, even_ref, odd_ref, part_ref):
    me, _ = place()
    own = rhs_ref.shape[1]
    rows = even_ref.shape[0] - rhs_ref.shape[0]

    def side(cols):
        pad = jnp.zeros((rows - 2, STRIP), F32)
        return jnp.concatenate([rhs_ref[:, cols], cvec_ref[:, cols], mass_ref[:, cols], pad], 0)

    put_sides(even_ref, odd_ref, side(slice(0, STRIP)), side(slice(own - STRIP, own)))
    part = rowsum(rhs_ref[...] * cvec_ref[...])
    part_ref[...] = rows_of([(me, part)], n)[: part_ref.shape[0]]


def build_kernel(rows_s, rows_v, lane_v, weight_v, o_ref, deg_ref, acc, merged):
    own, sub = o_ref.shape
    edges = merged.shape[0]
    blocks = edges // LANES
    panels = sub // LANES
    tall = 256

    def clear(i, _):
        acc[pl.ds(pl.multiple_of(i * tall, tall), tall), :] = jnp.zeros((tall, LANES), F32)
        return 0

    lax.fori_loop(0, panels * own // tall, clear, 0)

    fill = up(blocks, LANES) - blocks
    turned = jnp.transpose(
        jnp.concatenate([rows_v[...], jnp.zeros((fill, LANES), jnp.int32)], 0)
    )
    square = (LANES, LANES)
    down, across = iota(square, 0), iota(square, 1)
    same_group = (down // GROUP) == (across // GROUP)
    for k in range(blocks):
        equal = jnp.broadcast_to(turned[:, k : k + 1], square) == jnp.broadcast_to(
            rows_v[k : k + 1, :], square
        )
        equal = jnp.where(equal & same_group, 1.0, 0.0).astype(BF16)
        hit = down == jnp.broadcast_to(lane_v[k : k + 1, :], square)
        weight = weight_v[k : k + 1, :]
        high = weight.astype(BF16).astype(F32)
        total = None
        for part in (high, weight - high):
            spread = jnp.where(hit, jnp.broadcast_to(part, square), 0.0).astype(BF16)
            term = lax.dot_general(equal, spread, NT, preferred_element_type=F32)
            total = term if total is None else total + term
        merged[k * LANES : (k + 1) * LANES, :] = total

    def add(g, _):
        base = g * GROUP
        at = [rows_s[base + i] for i in range(GROUP)]
        new = merged[pl.ds(pl.multiple_of(base, GROUP), GROUP), :]
        old = [acc[pl.ds(r, 1), :] for r in at]
        out = [old[i] + new[i : i + 1, :] for i in range(GROUP)]
        for i in range(GROUP):
            acc[pl.ds(at[i], 1), :] = out[i]
        return 0

    lax.fori_loop(0, edges // GROUP, add, 0)

    def narrow(i, _):
        for p in range(panels):
            o_ref[pl.ds(pl.multiple_of(i * tall, tall), tall), p * LANES : (p + 1) * LANES] = acc[
                pl.ds(pl.multiple_of(p * own + i * tall, tall), tall), :
            ].astype(BF16)
        return 0

    lax.fori_loop(0, own // tall, narrow, 0)
    ones = jnp.ones((16, sub), BF16)
    through(deg_ref, ones, o_ref)


def through(out_ref, v, o_ref):
    own, sub = o_ref.shape
    tall = 256
    mine = v[:, STRIP : STRIP + own]

    for j in range(sub // tall):
        cols = slice(j * tall, (j + 1) * tall)
        out_ref[:, cols] = lax.dot_general(mine, o_ref[:, cols], NN, preferred_element_type=F32)
    for j in range(own // tall):
        cols = slice(STRIP + j * tall, STRIP + (j + 1) * tall)
        out_ref[:, cols] += lax.dot_general(
            v, o_ref[j * tall : (j + 1) * tall, :], NT, preferred_element_type=F32
        )


def local_solve(u_ref, wide, inv_ref):
    sub = u_ref.shape[1]
    tall = 256
    for j in range(sub // tall):
        cols = slice(j * tall, (j + 1) * tall)
        u_ref[:, cols] = jnp.dot(wide, inv_ref[:, cols], preferred_element_type=F32)


def put_strips(even_ref, odd_ref, ref):
    width = even_ref.shape[1]
    sub = ref.shape[1]
    put_sides(
        even_ref, odd_ref, ref[:, 0:width].astype(BF16), ref[:, sub - width :].astype(BF16)
    )


def first_solve_kernel(rhs_ref, even_got, odd_got, inv_ref, u_ref, even_ref, odd_ref):
    rhs = rhs_ref.shape[0]
    left, right = take_sides(even_got[0:rhs, :], odd_got[0:rhs, :])
    wide = jnp.concatenate([left, rhs_ref[...], right], 1).astype(BF16)
    local_solve(u_ref, wide, inv_ref)
    put_strips(even_ref, odd_ref, u_ref)


def next_solve_kernel(n, part_ref, even_got, odd_got, inv_ref, y_ref, u_ref, even_ref, odd_ref):
    left, right = take_sides(even_got[...], odd_got[...])
    wide = jnp.concatenate(widen(part_ref, left, right, n, None), 1)
    sub = wide.shape[1]
    y_ref[...] = wide[:, STRIP : sub - STRIP]
    local_solve(u_ref, wide.astype(BF16), inv_ref)
    put_strips(even_ref, odd_ref, u_ref)


def apply_common(
    n, u_ref, even_got, odd_got, halo_even, halo_odd, o_ref, deg_ref, sums_ref, cinv_ref, cvec_ref,
    mass_ref, wide_ref, out_ref,
):
    me, _ = place()
    rhs, sub = u_ref.shape
    own = sub - 2 * STRIP
    left, right = take_sides(even_got[...], odd_got[...])
    vec_left, vec_right = take_sides(halo_even[rhs : rhs + 1, :], halo_odd[rhs : rhs + 1, :])
    pick = jnp.where(
        (iota((n, LANES), 0) == me - 1 + iota((n, LANES), 1)) & (iota((n, LANES), 1) < 3), 1.0, 0.0
    )
    columns = jnp.dot(cinv_ref[...], pick, precision=HIGHEST, preferred_element_type=F32)
    coarse = lax.dot_general(
        sums_ref[0:n, :], columns, TN, precision=HIGHEST, preferred_element_type=F32
    )
    cvec = jnp.concatenate([vec_left, cvec_ref[...], vec_right], 1)
    parts = jnp.concatenate(widen(u_ref, left, right, n, None), 1)
    for j in range(sub // LANES):
        which = 0 if j == 0 else (2 if j == sub // LANES - 1 else 1)
        cols = slice(j * LANES, (j + 1) * LANES)
        wide_ref[:, cols] = parts[:, cols] + coarse[:, which : which + 1] * cvec[:, cols]
    wide = wide_ref[...]
    through(out_ref, wide.astype(BF16), o_ref)
    out_ref[...] = wide * deg_ref[0:1, :] - out_ref[...]
    out_ref[:, STRIP : STRIP + own] += mass_ref[...] * wide[:, STRIP : STRIP + own]
    return cvec


def first_apply_kernel(
    n, u_ref, even_got, odd_got, halo_even, halo_odd, o_ref, deg_ref, sums_ref, cinv_ref, cvec_ref,
    mass_ref, rhs_ref, z_ref, y_ref, even_ref, odd_ref, part_ref, wide_ref,
):
    me, _ = place()
    cvec = apply_common(
        n, u_ref, even_got, odd_got, halo_even, halo_odd, o_ref, deg_ref, sums_ref, cinv_ref,
        cvec_ref, mass_ref, wide_ref, y_ref,
    )
    sub = u_ref.shape[1]
    z_ref[...] = wide_ref[:, STRIP : sub - STRIP]
    put_strips(even_ref, odd_ref, y_ref)
    scaled = y_ref[...] * cvec
    a = rowsum(rhs_ref[...] * z_ref[...])
    b = rowsum(wide_ref[...] * y_ref[...])
    slots = up(n, 8)
    part_ref[0:slots, :] = rows_of(
        [
            (me - 1, rowsum(scaled[:, 0:STRIP])),
            (me, rowsum(scaled[:, STRIP : sub - STRIP])),
            (me + 1, rowsum(scaled[:, sub - STRIP :])),
        ],
        slots,
    )[0:slots]
    part_ref[slots : slots + 8, :] = rows_of([(0, a), (1, b)], 8)[0:8]


def next_apply_kernel(
    n, u_ref, even_got, odd_got, halo_even, halo_odd, o_ref, deg_ref, sums_ref, cinv_ref, cvec_ref,
    mass_ref, rhs_ref, y_ref, w_ref, q_ref, even_ref, odd_ref, part_ref, wide_ref, out_ref,
):
    apply_common(
        n, u_ref, even_got, odd_got, halo_even, halo_odd, o_ref, deg_ref, sums_ref, cinv_ref,
        cvec_ref, mass_ref, wide_ref, out_ref,
    )
    sub = u_ref.shape[1]
    w_ref[...] = wide_ref[:, STRIP : sub - STRIP]
    q_ref[...] = out_ref[:, STRIP : sub - STRIP]
    put_strips(even_ref, odd_ref, out_ref)
    c = rowsum(rhs_ref[...] * w_ref[...])
    d = rowsum(y_ref[...] * w_ref[...])
    e = rowsum(wide_ref[...] * out_ref[...])
    part_ref[...] = rows_of([(0, c), (1, d), (2, e)], 8)[0:8]


def finish_kernel(
    n, rhs_ref, z_ref, y_ref, w_ref, q_ref, even_got, odd_got, first_ref, second_ref, x_ref, r_ref
):
    slots = up(n, 8)
    a, b = first_ref[slots : slots + 1, :], first_ref[slots + 1 : slots + 2, :]
    c, d, e = second_ref[0:1, :], second_ref[1:2, :], second_ref[2:3, :]
    alpha = a / b
    following = a - alpha * (c + b) + alpha * alpha * d
    beta = following / a
    cross = b - alpha * d
    energy = (b - 2.0 * alpha * d + alpha * alpha * e) + 2.0 * beta * cross + beta * beta * b
    step = following / energy
    rhs, own = rhs_ref.shape
    near = jnp.transpose(jnp.broadcast_to(alpha + step * (1.0 + beta), (LANES, rhs)))[:, 0:1]
    far = jnp.transpose(jnp.broadcast_to(alpha * step, (LANES, rhs)))[:, 0:1]
    x_ref[...] = near * z_ref[...] - far * w_ref[...]
    left, right = take_sides(even_got[...], odd_got[...])
    r_ref[...] = rhs_ref[...] - near * y_ref[...] + far * q_ref[...]
    r_ref[:, 0:STRIP] += far * left
    r_ref[:, own - STRIP :] += far * right


def call(kernel, outs, scratch, limit, in_specs=None, count=None):
    vmem = pl.BlockSpec(memory_space=pltpu.VMEM)
    return pl.pallas_call(
        kernel,
        out_shape=[jax.ShapeDtypeStruct(s, d) for s, d in outs],
        in_specs=in_specs if in_specs is not None else [vmem] * count,
        out_specs=[vmem] * len(outs),
        scratch_shapes=scratch,
        compiler_params=pltpu.CompilerParams(vmem_limit_bytes=limit << 20),
    )


def swap(pair):
    n = lax.axis_size("tile")
    got = []
    for start, payload in zip((0, 1), pair):
        links = []
        for i in range(start, n - 1, 2):
            links += [(i, i + 1), (i + 1, i)]
        got.append(lax.ppermute(payload, "tile", links))
    return got


def total(part):
    n = lax.axis_size("tile")
    if n & (n - 1):
        return lax.psum(part, "tile")
    hop = 1
    while hop < n:
        part = part + lax.ppermute(part, "tile", [(i, i ^ hop) for i in range(n)])
        hop *= 2
    return part


def shards(
    rhs, mass_diag, edge_heads, edge_tails, edge_weight, local_inverse, coarse_vec, coarse_inv
):
    n = lax.axis_size("tile")
    rows, own = rhs.shape
    sub = local_inverse.shape[1]
    edges = edge_heads.shape[0]
    slots = up(n, 8)
    cvec, mass = coarse_vec[None, :], mass_diag[None, :]
    vmem = pl.BlockSpec(memory_space=pltpu.VMEM)
    smem = pl.BlockSpec(memory_space=pltpu.SMEM)

    side = ((rows + 8, STRIP), F32)
    even, odd, part = call(
        functools.partial(begin_kernel, n), [side, side, ((slots, rows), F32)], [], 4, count=3
    )(rhs, cvec, mass)
    halo = swap((even, odd))
    sums = total(part)

    at = (edge_tails >> 7) * own + (edge_heads - STRIP)
    shape = (edges // LANES, LANES)
    stiff, degree = call(
        build_kernel,
        [((own, sub), BF16), ((16, sub), F32)],
        [pltpu.VMEM((sub // LANES * own, LANES), F32), pltpu.VMEM((edges, LANES), F32)],
        32,
        in_specs=[smem, vmem, vmem, vmem],
    )(at, at.reshape(shape), (edge_tails & 127).reshape(shape), edge_weight.reshape(shape))

    whole, owned = ((rows, sub), F32), ((rows, own), F32)
    strip = ((rows, 2 * STRIP), BF16)
    u, even, odd = call(first_solve_kernel, [whole, strip, strip], [], 12, count=4)(
        rhs, *halo, local_inverse
    )
    got = swap((even, odd))
    z, y_part, even, odd, part = call(
        functools.partial(first_apply_kernel, n),
        [owned, whole, strip, strip, ((slots + 8, rows), F32)],
        [pltpu.VMEM((rows, sub), F32)],
        12,
        count=12,
    )(u, *got, *halo, stiff, degree, sums, coarse_inv, cvec, mass, rhs)
    got = swap((even, odd))
    first = total(part)
    y, u, even, odd = call(
        functools.partial(next_solve_kernel, n), [owned, whole, strip, strip], [], 12, count=4
    )(y_part, *got, local_inverse)
    got = swap((even, odd))
    strip = ((rows, STRIP), BF16)
    w, q, even, odd, part = call(
        functools.partial(next_apply_kernel, n),
        [owned, owned, strip, strip, ((8, rows), F32)],
        [pltpu.VMEM((rows, sub), F32), pltpu.VMEM((rows, sub), F32)],
        12,
        count=13,
    )(u, *got, *halo, stiff, degree, first, coarse_inv, cvec, mass, rhs, y)
    got = swap((even, odd))
    second = total(part)
    return tuple(
        call(functools.partial(finish_kernel, n), [owned, owned], [], 16, count=9)(
            rhs, z, y, w, q, *got, first, second
        )
    )


def solution(mesh):
    return jax.shard_map(
        shards,
        mesh=mesh,
        in_specs=(
            P("grp", "tile"),
            P("tile"),
            P("tile"),
            P("tile"),
            P("tile"),
            P("tile", None),
            P("tile"),
            P(),
        ),
        out_specs=(P("grp", "tile"), P("grp", "tile")),
        check_vma=False,
    )
```

```python
import functools

import jax
import jax.numpy as jnp
from jax import lax
from jax.experimental import pallas as pl
from jax.experimental.pallas import tpu as pltpu
from jax.sharding import PartitionSpec as P

STRIP = 128
LANES = 128
GROUP = 8
TURNS = 16
EXTRA = 16
F32 = jnp.float32
BF16 = jnp.bfloat16
NN = (((1,), (0,)), ((), ()))
NT = (((1,), (1,)), ((), ()))
TN = (((0,), (0,)), ((), ()))
HIGHEST = lax.Precision.HIGHEST


def up(value, unit):
    return -(-value // unit) * unit


def iota(shape, dim):
    return lax.broadcasted_iota(jnp.int32, shape, dim)


def place():
    me = lax.axis_index("tile").astype(jnp.int32)
    return me, lax.rem(me, jnp.int32(2)) == 0


def ends(n):
    me, _ = place()
    return (
        jnp.where(me > 0, 1.0, 0.0).astype(F32),
        jnp.where(me < n - 1, 1.0, 0.0).astype(F32),
    )


def put_sides(even_ref, odd_ref, left, right):
    _, even = place()

    @pl.when(even)
    def _():
        even_ref[...] = right
        odd_ref[...] = left

    @pl.when(jnp.logical_not(even))
    def _():
        even_ref[...] = left
        odd_ref[...] = right


def take_sides(even_got, odd_got):
    _, even = place()
    flag = jnp.where(even, 1.0, 0.0).astype(F32)
    a, b = even_got.astype(F32), odd_got.astype(F32)
    return jnp.where(flag > 0, b, a), jnp.where(flag > 0, a, b)


def flat(ref):
    return jnp.concatenate([ref[i : i + 1, :] for i in range(ref.shape[0])], 1)


def widen(own, got_left, got_right, n):
    first, last = ends(n)
    w = STRIP
    sub = own.shape[1]
    return jnp.concatenate(
        [
            (own[:, 0:w] + got_left[:, 0:w]) * first,
            own[:, w : 2 * w] + got_left[:, w:],
            own[:, 2 * w : sub - 2 * w],
            own[:, sub - 2 * w : sub - w] + got_right[:, 0:w],
            (own[:, sub - w :] + got_right[:, w:]) * last,
        ],
        1,
    )


def rows_of(columns, count):
    rhs = columns[0][1].shape[0]
    wide = up(count, LANES)
    lane = iota((rhs, wide), 1)
    total = jnp.zeros((rhs, wide), F32)
    for slot, column in columns:
        total = total + jnp.where(lane == slot, jnp.broadcast_to(column, (rhs, wide)), 0.0)
    return jnp.transpose(total)[0:count]


def rowsum(x):
    return jnp.sum(x, axis=1, keepdims=True)


def coarse_columns(n, sums, cinv_ref, reach):
    me, _ = place()
    shape = (n, LANES)
    lane = iota(shape, 1)
    pick = (iota(shape, 0) == me - reach + lane) & (lane <= 2 * reach)
    columns = jnp.dot(
        cinv_ref[...], jnp.where(pick, 1.0, 0.0), precision=HIGHEST, preferred_element_type=F32
    )
    return lax.dot_general(sums, columns, TN, precision=HIGHEST, preferred_element_type=F32)


def begin_kernel(n, rhs_ref, cvec_ref, even_ref, odd_ref, part_ref):
    me, _ = place()
    rhs, own = rhs_ref.shape
    slots = part_ref.shape[0]
    cvec = flat(cvec_ref)
    part = rows_of([(me, rowsum(rhs_ref[...] * cvec))], slots)
    part_ref[...] = part

    def side(start):
        pad = jnp.zeros((7, STRIP), F32)
        cols = slice(start, start + STRIP)
        return jnp.concatenate([rhs_ref[:, cols], cvec[:, cols], pad, part], 0)

    put_sides(even_ref, odd_ref, side(0), side(own - STRIP))


def build_kernel(rows_s, rows_v, lane_v, weight_v, o_ref, *scratch):
    merged, tables = scratch[0], scratch[1:]
    own, sub = o_ref.shape
    edges = merged.shape[0]
    blocks = edges // LANES
    panels = sub // LANES
    height = panels * own
    chunk = up(-(-height // blocks), 8)

    fill = up(blocks, LANES) - blocks
    turned = jnp.transpose(
        jnp.concatenate([rows_v[...], jnp.zeros((fill, LANES), jnp.int32)], 0)
    )
    square = (LANES, LANES)
    down, across = iota(square, 0), iota(square, 1)
    same_group = (down // GROUP) == (across // GROUP)
    for k in range(blocks):
        low = min(k * chunk, height)
        high = min(low + chunk, height)
        if high > low:
            for acc in tables:
                acc[low:high, :] = jnp.zeros((high - low, LANES), F32)
        equal = jnp.broadcast_to(turned[:, k : k + 1], square) == jnp.broadcast_to(
            rows_v[k : k + 1, :], square
        )
        equal = jnp.where(equal & same_group, 1.0, 0.0).astype(BF16)
        hit = down == jnp.broadcast_to(lane_v[k : k + 1, :], square)
        spread = jnp.where(hit, jnp.broadcast_to(weight_v[k : k + 1, :], square), 0.0)
        merged[k * LANES : (k + 1) * LANES, :] = lax.dot_general(
            equal, spread.astype(BF16), NT, preferred_element_type=F32
        )

    def add(g, _):
        for q in range(TURNS):
            acc = tables[q % len(tables)]
            base = (g * TURNS + q) * GROUP
            at = [rows_s[base + i] for i in range(GROUP)]
            new = merged[pl.ds(pl.multiple_of(base, GROUP), GROUP), :]
            out = [acc[pl.ds(at[i], 1), :] + new[i : i + 1, :] for i in range(GROUP)]
            for i in range(GROUP):
                acc[pl.ds(at[i], 1), :] = out[i]
        return 0

    lax.fori_loop(0, edges // (GROUP * TURNS), add, 0)

    tall = 256

    def narrow(i, _):
        for p in range(panels):
            rows = pl.ds(pl.multiple_of(p * own + i * tall, tall), tall)
            value = tables[0][rows, :]
            for acc in tables[1:]:
                value = value + acc[rows, :]
            o_ref[pl.ds(pl.multiple_of(i * tall, tall), tall), p * LANES : (p + 1) * LANES] = (
                value.astype(BF16)
            )
        return 0

    lax.fori_loop(0, own // tall, narrow, 0)


def local_solve(u_ref, wide, inv_ref):
    tall = 256
    for j in range(u_ref.shape[1] // tall):
        cols = slice(j * tall, (j + 1) * tall)
        u_ref[:, cols] = jnp.dot(wide, inv_ref[:, cols], preferred_element_type=F32)


def put_strips(even_ref, odd_ref, ref):
    width = even_ref.shape[1]
    sub = ref.shape[1]
    put_sides(
        even_ref, odd_ref, ref[:, 0:width].astype(BF16), ref[:, sub - width :].astype(BF16)
    )


def first_solve_kernel(
    rhs_ref, even_got, odd_got, inv_ref, sum_ref, sum_got, u_ref, even_ref, odd_ref, sum_out
):
    rhs = rhs_ref.shape[0]
    left, right = take_sides(even_got[0:rhs, :], odd_got[0:rhs, :])
    wide = jnp.concatenate([left, rhs_ref[...], right], 1).astype(BF16)
    local_solve(u_ref, wide, inv_ref)
    put_strips(even_ref, odd_ref, u_ref)
    sum_out[...] = sum_ref[...] + sum_got[...]


def product(wide_ref, o_ref, deg, mass, out_ref):
    rows, sub = wide_ref.shape
    own = sub - 2 * STRIP
    tall = 256
    high = wide_ref[...].astype(BF16)
    mine = high[:, STRIP : STRIP + own]
    sides = jnp.concatenate([o_ref[:, 0:STRIP], o_ref[:, sub - STRIP :]], 1)
    thru = lax.dot_general(mine, sides, NN, preferred_element_type=F32)
    for part, start in ((thru[:, 0:STRIP], 0), (thru[:, STRIP:], sub - STRIP)):
        cols = slice(start, start + STRIP)
        out_ref[:, cols] = wide_ref[:, cols] * deg(part, cols) - part
    for j in range(own // tall):
        cols = slice(STRIP + j * tall, STRIP + (j + 1) * tall)
        part = lax.dot_general(mine, o_ref[:, cols], NN, preferred_element_type=F32)
        part = part + lax.dot_general(
            high, o_ref[j * tall : (j + 1) * tall, :], NT, preferred_element_type=F32
        )
        diag = deg(part, cols) + mass[:, j * tall : (j + 1) * tall]
        out_ref[:, cols] = wide_ref[:, cols] * diag - part


def first_apply_kernel(
    n, u_ref, even_got, odd_got, halo_even, halo_odd, o_ref, cvec_ref, mass_ref, sum_ref, sum_got,
    s_ref, y_ref, deg_ref, even_ref, odd_ref, sum_out, wide_ref,
):
    rhs, sub = u_ref.shape
    own = sub - 2 * STRIP
    left, right = take_sides(even_got[...], odd_got[...])
    vec_left, vec_right = take_sides(halo_even[rhs : rhs + 1, :], halo_odd[rhs : rhs + 1, :])
    wide_ref[0:rhs, :] = widen(u_ref, left, right, n)
    cvec = jnp.concatenate([vec_left, flat(cvec_ref), vec_right], 1)
    lane = iota((1, sub), 1)
    wide_ref[rhs:, :] = jnp.concatenate(
        [
            jnp.where(lane < STRIP, cvec, 0.0),
            jnp.where((lane >= STRIP) & (lane < STRIP + own), cvec, 0.0),
            jnp.where(lane >= STRIP + own, cvec, 0.0),
            jnp.ones((1, sub), F32),
            jnp.zeros((EXTRA - 4, sub), F32),
        ],
        0,
    )

    def degree(part, cols):
        row = part[rhs + 3 : rhs + 4, :]
        deg_ref[:, cols] = jnp.broadcast_to(row, (8, row.shape[1]))
        return row

    product(wide_ref, o_ref, degree, flat(mass_ref), y_ref)
    s_ref[...] = wide_ref[0:rhs, STRIP : sub - STRIP]
    put_strips(even_ref, odd_ref, y_ref)
    sum_out[...] = sum_ref[...] + sum_got[...]


def add_coarse(value, vectors, coarse, first):
    for k in range(3):
        lane = first + k
        value = value + coarse[:, lane : lane + 1] * vectors[k : k + 1, :]
    return value


def next_solve_kernel(
    n, y_ref, even_got, odd_got, sums_ref, cinv_ref, inv_ref, own_ref, u_ref, even_ref, odd_ref
):
    rhs = u_ref.shape[0]
    sub = u_ref.shape[1]
    coarse = coarse_columns(n, sums_ref[0:n, :], cinv_ref, 2)
    left, right = take_sides(even_got[...], odd_got[...])
    left = add_coarse(left[0:rhs], left[rhs : rhs + 3], coarse, 0)
    right = add_coarse(right[0:rhs], right[rhs : rhs + 3], coarse, 2)
    value = add_coarse(y_ref[0:rhs, :], y_ref[rhs : rhs + 3, :], coarse, 1)
    wide = widen(value, left, right, n)
    own_ref[...] = wide[:, STRIP : sub - STRIP]
    local_solve(u_ref, wide.astype(BF16), inv_ref)
    put_strips(even_ref, odd_ref, u_ref)


def between_kernel(
    n, s_ref, y_ref, coarse_rows, even_got, odd_got, sums_ref, cinv_ref, cvec_ref, rhs_ref,
    z_ref, g_ref, part_ref,
):
    me, _ = place()
    rhs, own = s_ref.shape
    sub = own + 2 * STRIP
    slots = up(n, 8)
    coarse = coarse_columns(n, sums_ref[0:n, :], cinv_ref, 0)
    cvec = flat(cvec_ref)
    z = s_ref[...] + coarse[:, 0:1] * cvec
    z_ref[...] = z
    left, right = take_sides(even_got[rhs:, STRIP:], odd_got[rhs:, STRIP:])
    unused, right = take_sides(even_got[rhs:, 0:STRIP], odd_got[rhs:, 0:STRIP])
    mine = coarse_rows[rhs:, STRIP : sub - STRIP]
    lefts = [left[1:2, :], left[2:3, :], None]
    rights = [None, right[0:1, :], right[1:2, :]]
    rows = []
    for k in range(3):
        head, body, tail = (
            mine[k : k + 1, 0:STRIP],
            mine[k : k + 1, STRIP : own - STRIP],
            mine[k : k + 1, own - STRIP :],
        )
        if lefts[k] is not None:
            head = head + lefts[k]
        if rights[k] is not None:
            tail = tail + rights[k]
        rows.append(jnp.concatenate([head, body, tail], 1))
    g = jnp.concatenate(rows + [jnp.zeros((5, own), F32)], 0)
    g_ref[...] = g
    part_ref[0:slots, :] = rows_of([(me, rowsum(y_ref[...] * cvec))], slots)
    shape = (slots, rhs)
    here = iota(shape, 0) == me
    inner = rowsum(g * cvec)
    total = jnp.zeros(shape, F32)
    for k in range(3):
        take = here & (iota(shape, 1) == k)
        total = total + jnp.where(take, jnp.broadcast_to(inner[k : k + 1, :], shape), 0.0)
    part_ref[slots : 2 * slots, :] = total
    a, b = rowsum(rhs_ref[...] * s_ref[...]), rowsum(z * y_ref[...])
    part_ref[2 * slots :, :] = rows_of([(0, a), (1, b)], 8)


def next_apply_kernel(
    n, u_ref, even_got, odd_got, o_ref, deg_ref, mass_ref, rhs_ref, y_ref, g_ref, part_in,
    w_ref, q_ref, even_ref, odd_ref, part_ref, wide_ref, out_ref,
):
    me, _ = place()
    rhs, sub = u_ref.shape
    own = sub - 2 * STRIP
    slots = up(n, 8)
    left, right = take_sides(even_got[...], odd_got[...])
    wide_ref[...] = widen(u_ref, left, right, n)
    product(wide_ref, o_ref, lambda part, cols: deg_ref[0:1, cols], flat(mass_ref), out_ref)
    w = wide_ref[:, STRIP : sub - STRIP]
    w_ref[...] = w
    q_ref[...] = out_ref[:, STRIP : sub - STRIP]
    c = rowsum(rhs_ref[...] * w)
    d = rowsum(y_ref[...] * w)
    e = rowsum(wide_ref[...] * out_ref[...])
    cross = [(me - 1 + k, rowsum(w * g_ref[k : k + 1, :])) for k in range(3)]
    part_ref[0 : 2 * slots, :] = part_in[0 : 2 * slots, :]
    part_ref[2 * slots : 3 * slots, :] = rows_of(cross, slots)
    part_ref[3 * slots :, :] = part_in[2 * slots :, :] + rows_of([(2, c), (3, d), (4, e)], 8)
    _, even = place()

    @pl.when(even)
    def _():
        even_ref[0:rhs, :] = out_ref[:, sub - STRIP :]
        odd_ref[...] = out_ref[:, 0:STRIP]

    @pl.when(jnp.logical_not(even))
    def _():
        even_ref[0:rhs, :] = out_ref[:, 0:STRIP]
        odd_ref[...] = out_ref[:, sub - STRIP :]

    even_ref[rhs:, :] = part_ref[...]


def finish_kernel(
    n, rhs_ref, z_ref, y_ref, w_ref, q_ref, g_ref, even_got, odd_got, first_ref, part_ref,
    cinv_ref, cvec_ref, x_ref, r_ref,
):
    me, _ = place()
    rhs, own = rhs_ref.shape
    slots = up(n, 8)
    first = first_ref[0:n, :]
    rho, cross = part_ref[0:n, :], part_ref[2 * slots : 2 * slots + n, :]
    gram = part_ref[slots : slots + n, :]
    sums = part_ref[3 * slots :, :]
    exact = dict(precision=HIGHEST, preferred_element_type=F32)

    def over(x):
        return jnp.sum(x, axis=0, keepdims=True)

    start = lax.dot_general(cinv_ref[...], first, TN, **exact)
    level = lax.dot_general(cinv_ref[...], rho, TN, **exact)
    shape = (n, n)
    band = jnp.zeros(shape, F32)
    for k in range(3):
        take = iota(shape, 1) == iota(shape, 0) + (k - 1)
        band = band + jnp.where(take, jnp.broadcast_to(gram[:, k : k + 1], shape), 0.0)
    bent = jnp.dot(band, level, **exact)

    a = sums[0:1, :] + over(start * first)
    b = sums[1:2, :]
    c = sums[2:3, :] + over(level * first)
    d = sums[3:4, :] + over(level * rho)
    e = sums[4:5, :] + over(level * (2.0 * cross + bent))
    alpha = a / b
    following = a - alpha * (c + b) + alpha * alpha * d
    beta = following / a
    between = b - alpha * d
    energy = (b - 2.0 * alpha * d + alpha * alpha * e) + 2.0 * beta * between + beta * beta * b
    step = following / energy
    near = jnp.transpose(jnp.broadcast_to(alpha + step * (1.0 + beta), (LANES, rhs)))[:, 0:1]
    far = jnp.transpose(jnp.broadcast_to(alpha * step, (LANES, rhs)))[:, 0:1]
    coarse = coarse_columns(n, rho, cinv_ref, 1) * far
    x_ref[...] = near * z_ref[...] - far * w_ref[...] - coarse[:, 1:2] * flat(cvec_ref)
    left, right = take_sides(even_got[0:rhs, :], odd_got[...])
    r_ref[...] = add_coarse(
        rhs_ref[...] - near * y_ref[...] + far * q_ref[...], g_ref[...], coarse, 0
    )
    r_ref[:, 0:STRIP] += far * left
    r_ref[:, own - STRIP :] += far * right


def call(kernel, name, outs, scratch, limit, count, in_specs=None, flops=0):
    vmem = pl.BlockSpec(memory_space=pltpu.VMEM)
    return pl.pallas_call(
        kernel,
        out_shape=[jax.ShapeDtypeStruct(s, d) for s, d in outs],
        in_specs=in_specs if in_specs is not None else [vmem] * count,
        out_specs=[vmem] * len(outs),
        scratch_shapes=scratch,
        compiler_params=pltpu.CompilerParams(vmem_limit_bytes=limit << 20),
        cost_estimate=pl.CostEstimate(flops=flops, bytes_accessed=0, transcendentals=0),
        name=name,
    )


def swap(pair):
    n = lax.axis_size("tile")
    got = []
    for start, payload in zip((0, 1), pair):
        links = []
        for i in range(start, n - 1, 2):
            links += [(i, i + 1), (i + 1, i)]
        got.append(lax.ppermute(payload, "tile", links))
    return got


def across(part, hop):
    n = lax.axis_size("tile")
    if hop >= n:
        return jnp.zeros_like(part)
    return lax.ppermute(part, "tile", [(i, i ^ hop) for i in range(n)])


def finish_sum(part, hop):
    while hop < lax.axis_size("tile"):
        part = part + across(part, hop)
        hop *= 2
    return part


def shards(
    rhs, mass_diag, edge_heads, edge_tails, edge_weight, local_inverse, coarse_vec, coarse_inv
):
    n = lax.axis_size("tile")
    if n < 2 or n & (n - 1):
        raise ValueError("tile axis")
    rows, own = rhs.shape
    sub = local_inverse.shape[1]
    edges = edge_heads.shape[0]
    slots = up(n, 8)
    cvec, mass = coarse_vec.reshape(-1, LANES), mass_diag.reshape(-1, LANES)
    vmem = pl.BlockSpec(memory_space=pltpu.VMEM)
    smem = pl.BlockSpec(memory_space=pltpu.SMEM)
    bind = functools.partial

    side = ((rows + 8 + slots, STRIP), F32)
    few = ((slots, rows), F32)
    even, odd, part = call(bind(begin_kernel, n), "begin", [side, side, few], [], 4, 2)(rhs, cvec)
    halo = swap((even, odd))
    part = part + halo[0][rows + 8 :]

    at = (edge_tails >> 7) * own + (edge_heads - STRIP)
    shape = (edges // LANES, LANES)
    (stiff,) = call(
        build_kernel,
        "build",
        [((own, sub), BF16)],
        [pltpu.VMEM((edges, LANES), F32)] + [pltpu.VMEM((sub // LANES * own, LANES), F32)] * 2,
        34,
        4,
        in_specs=[smem, vmem, vmem, vmem],
        flops=10**10,
    )(at, at.reshape(shape), (edge_tails & 127).reshape(shape), edge_weight.reshape(shape))

    whole, owned = ((rows, sub), F32), ((rows, own), F32)
    strip = ((rows, 2 * STRIP), BF16)
    extra = ((rows + EXTRA, sub), F32)
    u, even, odd, part = call(
        first_solve_kernel, "solve", [whole, strip, strip, few], [], 12, 6, flops=10**9
    )(rhs, *halo, local_inverse, part, across(part, 2))
    got = swap((even, odd))
    strips = ((rows + EXTRA, 2 * STRIP), BF16)
    s, y_part, degree, even, odd, part = call(
        bind(first_apply_kernel, n),
        "apply",
        [owned, extra, ((8, sub), F32), strips, strips, few],
        [pltpu.VMEM(*extra)],
        12,
        10,
        flops=2 * 10**9,
    )(u, *got, *halo, stiff, cvec, mass, part, across(part, 4))
    got_y = swap((even, odd))
    sums = finish_sum(part, 8)
    y, u, even, odd = call(
        bind(next_solve_kernel, n), "solve2", [owned, whole, strip, strip], [], 12, 6, flops=10**9
    )(y_part, *got_y, sums, coarse_inv, local_inverse)
    got = swap((even, odd))
    z, g, part = call(
        bind(between_kernel, n),
        "between",
        [owned, ((8, own), F32), ((2 * slots + 8, rows), F32)],
        [],
        8,
        9,
        flops=10**9,
    )(s, y, y_part, *got_y, sums, coarse_inv, cvec, rhs)
    many = 3 * slots + 8
    w, q, even, odd, part = call(
        bind(next_apply_kernel, n),
        "apply2",
        [owned, owned, ((rows + many, STRIP), F32), ((rows, STRIP), F32), ((many, rows), F32)],
        [pltpu.VMEM(*whole), pltpu.VMEM(*whole)],
        12,
        10,
        flops=2 * 10**9,
    )(u, *got, stiff, degree, mass, rhs, y, g, part)
    got = swap((even, odd))
    part = finish_sum(part + got[0][rows:], 2)
    return tuple(
        call(bind(finish_kernel, n), "finish", [owned, owned], [], 16, 12)(
            rhs, z, y, w, q, g, *got, sums, part, coarse_inv, cvec
        )
    )


def solution(mesh):
    return jax.shard_map(
        shards,
        mesh=mesh,
        in_specs=(
            P("grp", "tile"),
            P("tile"),
            P("tile"),
            P("tile"),
            P("tile"),
            P("tile", None),
            P("tile"),
            P(),
        ),
        out_specs=(P("grp", "tile"), P("grp", "tile")),
        check_vma=False,
    )
```

```python
import functools

import jax
import jax.numpy as jnp
from jax import lax
from jax.experimental import pallas as pl
from jax.experimental.pallas import tpu as pltpu
from jax.sharding import PartitionSpec as P

STRIP = 128
LANES = 128
GROUP = 8
TURNS = 16
EXTRA = 16
F32 = jnp.float32
BF16 = jnp.bfloat16
NN = (((1,), (0,)), ((), ()))
NT = (((1,), (1,)), ((), ()))
TN = (((0,), (0,)), ((), ()))
HIGHEST = lax.Precision.HIGHEST


def up(value, unit):
    return -(-value // unit) * unit


def iota(shape, dim):
    return lax.broadcasted_iota(jnp.int32, shape, dim)


def place():
    me = lax.axis_index("tile").astype(jnp.int32)
    return me, lax.rem(me, jnp.int32(2)) == 0


def ends(n):
    me, _ = place()
    return (
        jnp.where(me > 0, 1.0, 0.0).astype(F32),
        jnp.where(me < n - 1, 1.0, 0.0).astype(F32),
    )


def put_sides(even_ref, odd_ref, left, right):
    _, even = place()

    @pl.when(even)
    def _():
        even_ref[...] = right
        odd_ref[...] = left

    @pl.when(jnp.logical_not(even))
    def _():
        even_ref[...] = left
        odd_ref[...] = right


def take_sides(even_got, odd_got):
    _, even = place()
    flag = jnp.where(even, 1.0, 0.0).astype(F32)
    a, b = even_got.astype(F32), odd_got.astype(F32)
    return jnp.where(flag > 0, b, a), jnp.where(flag > 0, a, b)


def flat(ref):
    return jnp.concatenate([ref[i : i + 1, :] for i in range(ref.shape[0])], 1)


def widen(own, got_left, got_right, n):
    first, last = ends(n)
    w = STRIP
    sub = own.shape[1]
    return jnp.concatenate(
        [
            (own[:, 0:w] + got_left[:, 0:w]) * first,
            own[:, w : 2 * w] + got_left[:, w:],
            own[:, 2 * w : sub - 2 * w],
            own[:, sub - 2 * w : sub - w] + got_right[:, 0:w],
            (own[:, sub - w :] + got_right[:, w:]) * last,
        ],
        1,
    )


def rows_of(columns, count):
    rhs = columns[0][1].shape[0]
    wide = up(count, LANES)
    lane = iota((rhs, wide), 1)
    total = jnp.zeros((rhs, wide), F32)
    for slot, column in columns:
        total = total + jnp.where(lane == slot, jnp.broadcast_to(column, (rhs, wide)), 0.0)
    return jnp.transpose(total)[0:count]


def rowsum(x):
    return jnp.sum(x, axis=1, keepdims=True)


def coarse_columns(n, sums, cinv_ref, reach):
    me, _ = place()
    shape = (n, LANES)
    lane = iota(shape, 1)
    pick = (iota(shape, 0) == me - reach + lane) & (lane <= 2 * reach)
    columns = jnp.dot(
        cinv_ref[...], jnp.where(pick, 1.0, 0.0), precision=HIGHEST, preferred_element_type=F32
    )
    return lax.dot_general(sums, columns, TN, precision=HIGHEST, preferred_element_type=F32)


def begin_kernel(n, rhs_ref, cvec_ref, even_ref, odd_ref, part_ref):
    me, _ = place()
    rhs, own = rhs_ref.shape
    slots = part_ref.shape[0]
    cvec = flat(cvec_ref)
    part = rows_of([(me, rowsum(rhs_ref[...] * cvec))], slots)
    part_ref[...] = part

    def side(start):
        pad = jnp.zeros((7, STRIP), F32)
        cols = slice(start, start + STRIP)
        return jnp.concatenate([rhs_ref[:, cols], cvec[:, cols], pad, part], 0)

    put_sides(even_ref, odd_ref, side(0), side(own - STRIP))


def build_kernel(rows_s, rows_v, lane_v, weight_v, o_ref, token, *scratch):
    token[...] = jnp.zeros(token.shape, F32)
    merged, tables = scratch[0], scratch[1:]
    own, sub = o_ref.shape
    edges = merged.shape[0]
    blocks = edges // LANES
    panels = sub // LANES
    height = panels * own
    chunk = up(-(-height // blocks), 8)

    fill = up(blocks, LANES) - blocks
    turned = jnp.transpose(
        jnp.concatenate([rows_v[...], jnp.zeros((fill, LANES), jnp.int32)], 0)
    )
    square = (LANES, LANES)
    down, across = iota(square, 0), iota(square, 1)
    same_group = (down // GROUP) == (across // GROUP)
    for k in range(blocks):
        low = min(k * chunk, height)
        high = min(low + chunk, height)
        if high > low:
            for acc in tables:
                acc[low:high, :] = jnp.zeros((high - low, LANES), F32)
        equal = jnp.broadcast_to(turned[:, k : k + 1], square) == jnp.broadcast_to(
            rows_v[k : k + 1, :], square
        )
        equal = jnp.where(equal & same_group, 1.0, 0.0).astype(BF16)
        hit = down == jnp.broadcast_to(lane_v[k : k + 1, :], square)
        spread = jnp.where(hit, jnp.broadcast_to(weight_v[k : k + 1, :], square), 0.0)
        merged[k * LANES : (k + 1) * LANES, :] = lax.dot_general(
            equal, spread.astype(BF16), NT, preferred_element_type=F32
        )

    def add(g, _):
        for q in range(TURNS):
            acc = tables[q % len(tables)]
            base = (g * TURNS + q) * GROUP
            at = [rows_s[base + i] for i in range(GROUP)]
            new = merged[pl.ds(pl.multiple_of(base, GROUP), GROUP), :]
            out = [acc[pl.ds(at[i], 1), :] + new[i : i + 1, :] for i in range(GROUP)]
            for i in range(GROUP):
                acc[pl.ds(at[i], 1), :] = out[i]
        return 0

    lax.fori_loop(0, edges // (GROUP * TURNS), add, 0)

    tall = 256

    def narrow(i, _):
        for p in range(panels):
            rows = pl.ds(pl.multiple_of(p * own + i * tall, tall), tall)
            value = tables[0][rows, :]
            for acc in tables[1:]:
                value = value + acc[rows, :]
            o_ref[pl.ds(pl.multiple_of(i * tall, tall), tall), p * LANES : (p + 1) * LANES] = (
                value.astype(BF16)
            )
        return 0

    lax.fori_loop(0, own // tall, narrow, 0)


def local_solve(u_ref, wide, inv_ref):
    tall = 256
    for j in range(u_ref.shape[1] // tall):
        cols = slice(j * tall, (j + 1) * tall)
        u_ref[:, cols] = jnp.dot(wide, inv_ref[:, cols], preferred_element_type=F32)


def put_strips(even_ref, odd_ref, ref):
    width = even_ref.shape[1]
    sub = ref.shape[1]
    put_sides(
        even_ref, odd_ref, ref[:, 0:width].astype(BF16), ref[:, sub - width :].astype(BF16)
    )


def first_solve_kernel(rhs_ref, even_got, odd_got, inv_ref, token, u_ref, even_ref, odd_ref):
    rhs = rhs_ref.shape[0]
    left, right = take_sides(even_got[0:rhs, :], odd_got[0:rhs, :])
    wide = jnp.concatenate([left, rhs_ref[...], right], 1).astype(BF16)
    local_solve(u_ref, wide, inv_ref)
    put_strips(even_ref, odd_ref, u_ref)


def blocks_of(sub):
    own = sub - 2 * STRIP
    tall = 256
    return [None] + [slice(j * tall, (j + 1) * tall) for j in range(own // tall)]


def sides_of(ref, rows):
    sub = ref.shape[1]
    return jnp.concatenate([ref[rows, 0:STRIP], ref[rows, sub - STRIP :]], 1)


def inner_product(inner, o_ref, out_ref):
    own, sub = o_ref.shape
    rows = slice(STRIP, own - STRIP)
    for block in blocks_of(sub):
        if block is None:
            thru = lax.dot_general(inner, sides_of(o_ref, rows), NN, preferred_element_type=F32)
            out_ref[:, 0:STRIP] = thru[:, 0:STRIP]
            out_ref[:, sub - STRIP :] = thru[:, STRIP:]
            continue
        cols = slice(STRIP + block.start, STRIP + block.stop)
        part = lax.dot_general(inner, o_ref[rows, cols], NN, preferred_element_type=F32)
        out_ref[:, cols] = part + lax.dot_general(
            inner, o_ref[block, 2 * STRIP : sub - 2 * STRIP], NT, preferred_element_type=F32
        )


def outer_product(wide_ref, o_ref, thru_ref, deg, mass, out_ref):
    own, sub = o_ref.shape
    w = STRIP
    low, high = wide_ref[:, 0 : 2 * w].astype(BF16), wide_ref[:, sub - 2 * w :].astype(BF16)
    both = jnp.concatenate([low, high], 1)
    mine = jnp.concatenate([low[:, w:], high[:, 0:w]], 1)

    def rows(pick):
        return jnp.concatenate([pick(slice(0, w)), pick(slice(own - w, own))], 0)

    for block in blocks_of(sub):
        if block is None:
            part = lax.dot_general(
                mine, rows(lambda r: sides_of(o_ref, r)), NN, preferred_element_type=F32
            )
            for piece, start in ((part[:, 0:w], 0), (part[:, w:], sub - w)):
                cols = slice(start, start + w)
                piece = piece + thru_ref[:, cols]
                out_ref[:, cols] = wide_ref[:, cols] * deg(piece, cols) - piece
            continue
        cols = slice(w + block.start, w + block.stop)
        part = lax.dot_general(
            mine, rows(lambda r: o_ref[r, cols]), NN, preferred_element_type=F32
        )
        ends_of = jnp.concatenate([o_ref[block, 0 : 2 * w], o_ref[block, sub - 2 * w :]], 1)
        part = part + lax.dot_general(both, ends_of, NT, preferred_element_type=F32)
        part = part + thru_ref[:, cols]
        out_ref[:, cols] = wide_ref[:, cols] * (deg(part, cols) + mass[:, block]) - part


def fixed_rows(cvec, start, stop, sub):
    own = sub - 2 * STRIP
    lane = start + iota((1, stop - start), 1)
    return jnp.concatenate(
        [
            jnp.where(lane < STRIP, cvec, 0.0),
            jnp.where((lane >= STRIP) & (lane < STRIP + own), cvec, 0.0),
            jnp.where(lane >= STRIP + own, cvec, 0.0),
            jnp.ones(cvec.shape, F32),
            jnp.zeros((EXTRA - 4, stop - start), F32),
        ],
        0,
    )


def first_inner_kernel(u_ref, o_ref, cvec_ref, sum_ref, sum_got, thru_ref, sum_out):
    rhs, sub = u_ref.shape
    inner = slice(2 * STRIP, sub - 2 * STRIP)
    cvec = flat(cvec_ref)[:, STRIP : sub - 3 * STRIP]
    fixed = fixed_rows(cvec, inner.start, inner.stop, sub)
    value = jnp.concatenate([u_ref[:, inner], fixed], 0).astype(BF16)
    inner_product(value, o_ref, thru_ref)
    sum_out[...] = sum_ref[...] + sum_got[...]


def first_outer_kernel(
    n, u_ref, even_got, odd_got, halo_even, halo_odd, o_ref, thru_ref, cvec_ref, mass_ref,
    s_ref, y_ref, deg_ref, even_ref, odd_ref, wide_ref,
):
    rhs, sub = u_ref.shape
    left, right = take_sides(even_got[...], odd_got[...])
    vec_left, vec_right = take_sides(halo_even[rhs : rhs + 1, :], halo_odd[rhs : rhs + 1, :])
    wide_ref[0:rhs, :] = widen(u_ref, left, right, n)
    cvec = jnp.concatenate([vec_left, flat(cvec_ref), vec_right], 1)
    wide_ref[rhs:, :] = fixed_rows(cvec, 0, sub, sub)

    def degree(part, cols):
        row = part[rhs + 3 : rhs + 4, :]
        deg_ref[:, cols] = jnp.broadcast_to(row, (8, row.shape[1]))
        return row

    outer_product(wide_ref, o_ref, thru_ref, degree, flat(mass_ref), y_ref)
    s_ref[...] = wide_ref[0:rhs, STRIP : sub - STRIP]
    put_strips(even_ref, odd_ref, y_ref)


def add_coarse(value, vectors, coarse, first):
    for k in range(3):
        lane = first + k
        value = value + coarse[:, lane : lane + 1] * vectors[k : k + 1, :]
    return value


def solve_inner_kernel(n, y_ref, sums_ref, cinv_ref, inv_ref, own_ref, u_ref):
    rhs, sub = u_ref.shape
    inner = slice(2 * STRIP, sub - 2 * STRIP)
    coarse = coarse_columns(n, sums_ref[0:n, :], cinv_ref, 2)
    value = add_coarse(y_ref[0:rhs, inner], y_ref[rhs : rhs + 3, inner], coarse, 1)
    own_ref[...] = value
    high = value.astype(BF16)
    tall = 256
    for j in range(sub // tall):
        cols = slice(j * tall, (j + 1) * tall)
        u_ref[:, cols] = jnp.dot(high, inv_ref[inner, cols], preferred_element_type=F32)


def solve_outer_kernel(
    n, y_ref, even_got, odd_got, sums_ref, cinv_ref, inv_ref, inner_ref, half_ref,
    own_ref, u_ref, even_ref, odd_ref,
):
    rhs, sub = u_ref.shape
    w = STRIP
    first, last = ends(n)
    coarse = coarse_columns(n, sums_ref[0:n, :], cinv_ref, 2)
    left, right = take_sides(even_got[...], odd_got[...])
    left = add_coarse(left[0:rhs], left[rhs : rhs + 3], coarse, 0)
    right = add_coarse(right[0:rhs], right[rhs : rhs + 3], coarse, 2)
    low, high = slice(0, 2 * w), slice(sub - 2 * w, sub)
    left = left + add_coarse(y_ref[0:rhs, low], y_ref[rhs : rhs + 3, low], coarse, 1)
    right = right + add_coarse(y_ref[0:rhs, high], y_ref[rhs : rhs + 3, high], coarse, 1)
    own_ref[:, 0:w] = left[:, w:]
    own_ref[:, w : sub - 3 * w] = inner_ref[...]
    own_ref[:, sub - 3 * w :] = right[:, 0:w]
    both = jnp.concatenate(
        [left[:, 0:w] * first, left[:, w:], right[:, 0:w], right[:, w:] * last], 1
    ).astype(BF16)
    tall = 256
    for j in range(sub // tall):
        cols = slice(j * tall, (j + 1) * tall)
        part = jnp.concatenate([inv_ref[low, cols], inv_ref[high, cols]], 0)
        u_ref[:, cols] = half_ref[:, cols] + jnp.dot(both, part, preferred_element_type=F32)
    put_strips(even_ref, odd_ref, u_ref)


def between_kernel(
    n, s_ref, y_ref, coarse_rows, even_got, odd_got, sums_ref, cinv_ref, cvec_ref, rhs_ref,
    z_ref, g_ref, part_ref,
):
    me, _ = place()
    rhs, own = s_ref.shape
    sub = own + 2 * STRIP
    slots = up(n, 8)
    coarse = coarse_columns(n, sums_ref[0:n, :], cinv_ref, 0)
    cvec = flat(cvec_ref)
    z = s_ref[...] + coarse[:, 0:1] * cvec
    z_ref[...] = z
    left, right = take_sides(even_got[rhs:, STRIP:], odd_got[rhs:, STRIP:])
    unused, right = take_sides(even_got[rhs:, 0:STRIP], odd_got[rhs:, 0:STRIP])
    mine = coarse_rows[rhs:, STRIP : sub - STRIP]
    lefts = [left[1:2, :], left[2:3, :], None]
    rights = [None, right[0:1, :], right[1:2, :]]
    rows = []
    for k in range(3):
        head, body, tail = (
            mine[k : k + 1, 0:STRIP],
            mine[k : k + 1, STRIP : own - STRIP],
            mine[k : k + 1, own - STRIP :],
        )
        if lefts[k] is not None:
            head = head + lefts[k]
        if rights[k] is not None:
            tail = tail + rights[k]
        rows.append(jnp.concatenate([head, body, tail], 1))
    g = jnp.concatenate(rows + [jnp.zeros((5, own), F32)], 0)
    g_ref[...] = g
    part_ref[0:slots, :] = rows_of([(me, rowsum(y_ref[...] * cvec))], slots)
    shape = (slots, rhs)
    here = iota(shape, 0) == me
    inner = rowsum(g * cvec)
    total = jnp.zeros(shape, F32)
    for k in range(3):
        take = here & (iota(shape, 1) == k)
        total = total + jnp.where(take, jnp.broadcast_to(inner[k : k + 1, :], shape), 0.0)
    part_ref[slots : 2 * slots, :] = total
    a, b = rowsum(rhs_ref[...] * s_ref[...]), rowsum(z * y_ref[...])
    part_ref[2 * slots :, :] = rows_of([(0, a), (1, b)], 8)


def next_inner_kernel(u_ref, o_ref, rhs_ref, y_ref, g_ref, thru_ref, dots_ref):
    rhs, sub = u_ref.shape
    own = sub - 2 * STRIP
    value = u_ref[:, 2 * STRIP : sub - 2 * STRIP]
    inner_product(value.astype(BF16), o_ref, thru_ref)
    inner = slice(STRIP, own - STRIP)
    columns = [rowsum(value * rhs_ref[:, inner]), rowsum(value * y_ref[:, inner])]
    columns += [rowsum(value * g_ref[k : k + 1, inner]) for k in range(3)]
    lane = iota((rhs, LANES), 1)
    total = jnp.zeros((rhs, LANES), F32)
    for k, column in enumerate(columns):
        total = total + jnp.where(lane == k, jnp.broadcast_to(column, (rhs, LANES)), 0.0)
    dots_ref[...] = total


def next_outer_kernel(
    n, u_ref, even_got, odd_got, o_ref, thru_ref, dots_ref, deg_ref, mass_ref, rhs_ref, y_ref,
    g_ref, part_in, w_ref, q_ref, even_ref, odd_ref, part_ref, wide_ref, out_ref,
):
    me, even = place()
    rhs, sub = u_ref.shape
    own = sub - 2 * STRIP
    slots = up(n, 8)
    left, right = take_sides(even_got[...], odd_got[...])
    wide_ref[...] = widen(u_ref, left, right, n)
    outer_product(
        wide_ref, o_ref, thru_ref, lambda part, cols: deg_ref[0:1, cols], flat(mass_ref), out_ref
    )
    w_ref[...] = wide_ref[:, STRIP : sub - STRIP]
    q_ref[...] = out_ref[:, STRIP : sub - STRIP]
    e = rowsum(wide_ref[...] * out_ref[...])

    def edges_of(ref):
        return jnp.concatenate([ref[:, 0:STRIP], ref[:, own - STRIP :]], 1)

    w = jnp.concatenate(
        [wide_ref[:, STRIP : 2 * STRIP], wide_ref[:, sub - 2 * STRIP : sub - STRIP]], 1
    )
    g = edges_of(g_ref)
    c = dots_ref[:, 0:1] + rowsum(w * edges_of(rhs_ref))
    d = dots_ref[:, 1:2] + rowsum(w * edges_of(y_ref))
    cross = [
        (me - 1 + k, dots_ref[:, 2 + k : 3 + k] + rowsum(w * g[k : k + 1, :])) for k in range(3)
    ]
    part_ref[0 : 2 * slots, :] = part_in[0 : 2 * slots, :]
    part_ref[2 * slots : 3 * slots, :] = rows_of(cross, slots)
    part_ref[3 * slots :, :] = part_in[2 * slots :, :] + rows_of([(2, c), (3, d), (4, e)], 8)

    @pl.when(even)
    def _():
        even_ref[0:rhs, :] = out_ref[:, sub - STRIP :]
        odd_ref[...] = out_ref[:, 0:STRIP]

    @pl.when(jnp.logical_not(even))
    def _():
        even_ref[0:rhs, :] = out_ref[:, 0:STRIP]
        odd_ref[...] = out_ref[:, sub - STRIP :]

    even_ref[rhs:, :] = part_ref[...]


def finish_kernel(
    n, rhs_ref, z_ref, y_ref, w_ref, q_ref, g_ref, even_got, odd_got, first_ref, part_ref,
    cinv_ref, cvec_ref, x_ref, r_ref,
):
    me, _ = place()
    rhs, own = rhs_ref.shape
    slots = up(n, 8)
    first = first_ref[0:n, :]
    rho, cross = part_ref[0:n, :], part_ref[2 * slots : 2 * slots + n, :]
    gram = part_ref[slots : slots + n, :]
    sums = part_ref[3 * slots :, :]
    exact = dict(precision=HIGHEST, preferred_element_type=F32)

    def over(x):
        return jnp.sum(x, axis=0, keepdims=True)

    start = lax.dot_general(cinv_ref[...], first, TN, **exact)
    level = lax.dot_general(cinv_ref[...], rho, TN, **exact)
    shape = (n, n)
    band = jnp.zeros(shape, F32)
    for k in range(3):
        take = iota(shape, 1) == iota(shape, 0) + (k - 1)
        band = band + jnp.where(take, jnp.broadcast_to(gram[:, k : k + 1], shape), 0.0)
    bent = jnp.dot(band, level, **exact)

    a = sums[0:1, :] + over(start * first)
    b = sums[1:2, :]
    c = sums[2:3, :] + over(level * first)
    d = sums[3:4, :] + over(level * rho)
    e = sums[4:5, :] + over(level * (2.0 * cross + bent))
    alpha = a / b
    following = a - alpha * (c + b) + alpha * alpha * d
    beta = following / a
    between = b - alpha * d
    energy = (b - 2.0 * alpha * d + alpha * alpha * e) + 2.0 * beta * between + beta * beta * b
    step = following / energy
    near = jnp.transpose(jnp.broadcast_to(alpha + step * (1.0 + beta), (LANES, rhs)))[:, 0:1]
    far = jnp.transpose(jnp.broadcast_to(alpha * step, (LANES, rhs)))[:, 0:1]
    coarse = coarse_columns(n, rho, cinv_ref, 1) * far
    x_ref[...] = near * z_ref[...] - far * w_ref[...] - coarse[:, 1:2] * flat(cvec_ref)
    left, right = take_sides(even_got[0:rhs, :], odd_got[...])
    r_ref[...] = add_coarse(
        rhs_ref[...] - near * y_ref[...] + far * q_ref[...], g_ref[...], coarse, 0
    )
    r_ref[:, 0:STRIP] += far * left
    r_ref[:, own - STRIP :] += far * right


def call(kernel, name, outs, scratch, limit, count, in_specs=None, flops=0):
    vmem = pl.BlockSpec(memory_space=pltpu.VMEM)
    return pl.pallas_call(
        kernel,
        out_shape=[jax.ShapeDtypeStruct(s, d) for s, d in outs],
        in_specs=in_specs if in_specs is not None else [vmem] * count,
        out_specs=[vmem] * len(outs),
        scratch_shapes=scratch,
        compiler_params=pltpu.CompilerParams(vmem_limit_bytes=limit << 20),
        cost_estimate=pl.CostEstimate(flops=flops, bytes_accessed=0, transcendentals=0),
        name=name,
    )


def swap(pair):
    n = lax.axis_size("tile")
    got = []
    for start, payload in zip((0, 1), pair):
        links = []
        for i in range(start, n - 1, 2):
            links += [(i, i + 1), (i + 1, i)]
        got.append(lax.ppermute(payload, "tile", links))
    return got


def across(part, hop):
    n = lax.axis_size("tile")
    if hop >= n:
        return jnp.zeros_like(part)
    return lax.ppermute(part, "tile", [(i, i ^ hop) for i in range(n)])


def finish_sum(part, hop):
    while hop < lax.axis_size("tile"):
        part = part + across(part, hop)
        hop *= 2
    return part


def shards(
    rhs, mass_diag, edge_heads, edge_tails, edge_weight, local_inverse, coarse_vec, coarse_inv
):
    n = lax.axis_size("tile")
    if n < 2 or n & (n - 1):
        raise ValueError("tile axis")
    rows, own = rhs.shape
    sub = local_inverse.shape[1]
    edges = edge_heads.shape[0]
    slots = up(n, 8)
    cvec, mass = coarse_vec.reshape(-1, LANES), mass_diag.reshape(-1, LANES)
    vmem = pl.BlockSpec(memory_space=pltpu.VMEM)
    smem = pl.BlockSpec(memory_space=pltpu.SMEM)
    bind = functools.partial

    side = ((rows + 8 + slots, STRIP), F32)
    few = ((slots, rows), F32)
    even, odd, part = call(bind(begin_kernel, n), "begin", [side, side, few], [], 4, 2)(rhs, cvec)
    halo = swap((even, odd))
    part = part + halo[0][rows + 8 :]

    at = (edge_tails >> 7) * own + (edge_heads - STRIP)
    shape = (edges // LANES, LANES)
    stiff, token = call(
        build_kernel,
        "build",
        [((own, sub), BF16), ((8, LANES), F32)],
        [pltpu.VMEM((edges, LANES), F32)] + [pltpu.VMEM((sub // LANES * own, LANES), F32)] * 2,
        34,
        4,
        in_specs=[smem, vmem, vmem, vmem],
        flops=10**10,
    )(at, at.reshape(shape), (edge_tails & 127).reshape(shape), edge_weight.reshape(shape))
    part = part + across(part, 2)

    whole, owned = ((rows, sub), F32), ((rows, own), F32)
    strip = ((rows, 2 * STRIP), BF16)
    extra = ((rows + EXTRA, sub), F32)
    u, even, odd = call(
        first_solve_kernel, "solve", [whole, strip, strip], [], 12, 5, flops=10**9
    )(rhs, *halo, local_inverse, token)
    got = swap((even, odd))
    thru, part = call(first_inner_kernel, "inner", [extra, few], [], 8, 5, flops=2 * 10**9)(
        u, stiff, cvec, part, across(part, 4)
    )
    sums = finish_sum(part, 8)
    strips = ((rows + EXTRA, 2 * STRIP), BF16)
    s, y_part, degree, even, odd = call(
        bind(first_outer_kernel, n),
        "outer",
        [owned, extra, ((8, sub), F32), strips, strips],
        [pltpu.VMEM(*extra)],
        12,
        9,
        flops=10**9,
    )(u, *got, *halo, stiff, thru, cvec, mass)
    got_y = swap((even, odd))
    inner, half = call(
        bind(solve_inner_kernel, n),
        "solve_inner",
        [((rows, own - 2 * STRIP), F32), whole],
        [],
        8,
        4,
        flops=10**9,
    )(y_part, sums, coarse_inv, local_inverse)
    y, u, even, odd = call(
        bind(solve_outer_kernel, n),
        "solve_outer",
        [owned, whole, strip, strip],
        [],
        12,
        8,
        flops=10**8,
    )(y_part, *got_y, sums, coarse_inv, local_inverse, inner, half)
    got = swap((even, odd))
    z, g, part = call(
        bind(between_kernel, n),
        "between",
        [owned, ((8, own), F32), ((2 * slots + 8, rows), F32)],
        [],
        8,
        9,
        flops=10**9,
    )(s, y, y_part, *got_y, sums, coarse_inv, cvec, rhs)
    thru, dots = call(
        next_inner_kernel, "inner2", [whole, ((rows, LANES), F32)], [], 8, 5, flops=2 * 10**9
    )(u, stiff, rhs, y, g)
    many = 3 * slots + 8
    w, q, even, odd, part = call(
        bind(next_outer_kernel, n),
        "outer2",
        [owned, owned, ((rows + many, STRIP), F32), ((rows, STRIP), F32), ((many, rows), F32)],
        [pltpu.VMEM(*whole), pltpu.VMEM(*whole)],
        12,
        12,
        flops=10**9,
    )(u, *got, stiff, thru, dots, degree, mass, rhs, y, g, part)
    got = swap((even, odd))
    part = finish_sum(part + got[0][rows:], 2)
    return tuple(
        call(bind(finish_kernel, n), "finish", [owned, owned], [], 16, 12)(
            rhs, z, y, w, q, g, *got, sums, part, coarse_inv, cvec
        )
    )


def solution(mesh):
    return jax.shard_map(
        shards,
        mesh=mesh,
        in_specs=(
            P("grp", "tile"),
            P("tile"),
            P("tile"),
            P("tile"),
            P("tile"),
            P("tile", None),
            P("tile"),
            P(),
        ),
        out_specs=(P("grp", "tile"), P("grp", "tile")),
        check_vma=False,
    )
```

```python
import functools

import jax
import jax.numpy as jnp
from jax import lax
from jax.experimental import pallas as pl
from jax.experimental.pallas import tpu as pltpu
from jax.sharding import PartitionSpec as P

STRIP = 128
LANES = 128
GROUP = 8
TURNS = 16
EXTRA = 16
CHUNKS = 4
F32 = jnp.float32
BF16 = jnp.bfloat16
NN = (((1,), (0,)), ((), ()))
NT = (((1,), (1,)), ((), ()))
TN = (((0,), (0,)), ((), ()))
HIGHEST = lax.Precision.HIGHEST


def up(value, unit):
    return -(-value // unit) * unit


def iota(shape, dim):
    return lax.broadcasted_iota(jnp.int32, shape, dim)


def place():
    me = lax.axis_index("tile").astype(jnp.int32)
    return me, lax.rem(me, jnp.int32(2)) == 0


def ends(n):
    me, _ = place()
    return (
        jnp.where(me > 0, 1.0, 0.0).astype(F32),
        jnp.where(me < n - 1, 1.0, 0.0).astype(F32),
    )


def put_sides(even_ref, odd_ref, left, right):
    _, even = place()

    @pl.when(even)
    def _():
        even_ref[...] = right
        odd_ref[...] = left

    @pl.when(jnp.logical_not(even))
    def _():
        even_ref[...] = left
        odd_ref[...] = right


def take_sides(even_got, odd_got):
    _, even = place()
    flag = jnp.where(even, 1.0, 0.0).astype(F32)
    a, b = even_got.astype(F32), odd_got.astype(F32)
    return jnp.where(flag > 0, b, a), jnp.where(flag > 0, a, b)


def flat(ref):
    return jnp.concatenate([ref[i : i + 1, :] for i in range(ref.shape[0])], 1)


def widen(own, got_left, got_right, n):
    first, last = ends(n)
    w = STRIP
    sub = own.shape[1]
    return jnp.concatenate(
        [
            (own[:, 0:w] + got_left[:, 0:w]) * first,
            own[:, w : 2 * w] + got_left[:, w:],
            own[:, 2 * w : sub - 2 * w],
            own[:, sub - 2 * w : sub - w] + got_right[:, 0:w],
            (own[:, sub - w :] + got_right[:, w:]) * last,
        ],
        1,
    )


def rows_of(columns, count):
    rhs = columns[0][1].shape[0]
    wide = up(count, LANES)
    lane = iota((rhs, wide), 1)
    total = jnp.zeros((rhs, wide), F32)
    for slot, column in columns:
        total = total + jnp.where(lane == slot, jnp.broadcast_to(column, (rhs, wide)), 0.0)
    return jnp.transpose(total)[0:count]


def rowsum(x):
    return jnp.sum(x, axis=1, keepdims=True)


def coarse_columns(n, sums, cinv_ref, reach):
    me, _ = place()
    shape = (n, LANES)
    lane = iota(shape, 1)
    pick = (iota(shape, 0) == me - reach + lane) & (lane <= 2 * reach)
    columns = jnp.dot(
        cinv_ref[...], jnp.where(pick, 1.0, 0.0), precision=HIGHEST, preferred_element_type=F32
    )
    return lax.dot_general(sums, columns, TN, precision=HIGHEST, preferred_element_type=F32)


def begin_kernel(rhs_hbm, cvec_hbm, even_ref, odd_ref, part_ref, rhs_ref, cvec_ref, sem):
    me, _ = place()
    _, own = rhs_ref.shape
    slots = part_ref.shape[0]
    copies = [
        pltpu.make_async_copy(rhs_hbm, rhs_ref, sem.at[0]),
        pltpu.make_async_copy(cvec_hbm, cvec_ref, sem.at[1]),
    ]
    for copy in copies:
        copy.start()
    for copy in copies:
        copy.wait()
    cvec = flat(cvec_ref)
    part = rows_of([(me, rowsum(rhs_ref[...] * cvec))], slots)
    part_ref[...] = part

    def side(start):
        pad = jnp.zeros((7, STRIP), F32)
        cols = slice(start, start + STRIP)
        return jnp.concatenate([rhs_ref[:, cols], cvec[:, cols], pad, part], 0)

    put_sides(even_ref, odd_ref, side(0), side(own - STRIP))


def build_kernel(rows_s, rows_v, lane_v, weight_hbm, o_ref, token, weight_v, sem, *scratch):
    copy = pltpu.make_async_copy(weight_hbm, weight_v, sem)
    copy.start()
    token[...] = jnp.zeros(token.shape, F32)
    merged, tables = scratch[0], scratch[1:]
    own, sub = o_ref.shape
    edges = merged.shape[0]
    blocks = edges // LANES
    panels = sub // LANES
    height = panels * own
    chunk = up(-(-height // blocks), 8)

    fill = up(blocks, LANES) - blocks
    turned = jnp.transpose(
        jnp.concatenate([rows_v[...], jnp.zeros((fill, LANES), jnp.int32)], 0)
    )
    square = (LANES, LANES)
    down, across = iota(square, 0), iota(square, 1)
    same_group = (down // GROUP) == (across // GROUP)
    copy.wait()
    for k in range(blocks):
        low = min(k * chunk, height)
        high = min(low + chunk, height)
        if high > low:
            for acc in tables:
                acc[low:high, :] = jnp.zeros((high - low, LANES), F32)
        equal = jnp.broadcast_to(turned[:, k : k + 1], square) == jnp.broadcast_to(
            rows_v[k : k + 1, :], square
        )
        equal = jnp.where(equal & same_group, 1.0, 0.0).astype(BF16)
        hit = down == jnp.broadcast_to(lane_v[k : k + 1, :], square)
        spread = jnp.where(hit, jnp.broadcast_to(weight_v[k : k + 1, :], square), 0.0)
        merged[k * LANES : (k + 1) * LANES, :] = lax.dot_general(
            equal, spread.astype(BF16), NT, preferred_element_type=F32
        )

    def add(g, _):
        for q in range(TURNS):
            acc = tables[q % len(tables)]
            base = (g * TURNS + q) * GROUP
            at = [rows_s[base + i] for i in range(GROUP)]
            new = merged[pl.ds(pl.multiple_of(base, GROUP), GROUP), :]
            out = [acc[pl.ds(at[i], 1), :] + new[i : i + 1, :] for i in range(GROUP)]
            for i in range(GROUP):
                acc[pl.ds(at[i], 1), :] = out[i]
        return 0

    lax.fori_loop(0, edges // (GROUP * TURNS), add, 0)

    tall = 256

    def narrow(i, _):
        for p in range(panels):
            rows = pl.ds(pl.multiple_of(p * own + i * tall, tall), tall)
            value = tables[0][rows, :]
            for acc in tables[1:]:
                value = value + acc[rows, :]
            o_ref[pl.ds(pl.multiple_of(i * tall, tall), tall), p * LANES : (p + 1) * LANES] = (
                value.astype(BF16)
            )
        return 0

    lax.fori_loop(0, own // tall, narrow, 0)


def local_solve(u_ref, wide, inv_ref):
    tall = 256
    for j in range(u_ref.shape[1] // tall):
        cols = slice(j * tall, (j + 1) * tall)
        u_ref[:, cols] = jnp.dot(wide, inv_ref[:, cols], preferred_element_type=F32)


def put_strips(even_ref, odd_ref, ref):
    width = even_ref.shape[1]
    sub = ref.shape[1]
    put_sides(
        even_ref, odd_ref, ref[:, 0:width].astype(BF16), ref[:, sub - width :].astype(BF16)
    )


def first_solve_kernel(
    rhs_ref, even_got, odd_got, inv_ref, token, sum_ref, sum_got, u_ref, even_ref, odd_ref, sum_out
):
    rhs = rhs_ref.shape[0]
    left, right = take_sides(even_got[0:rhs, :], odd_got[0:rhs, :])
    wide = jnp.concatenate([left, rhs_ref[...], right], 1).astype(BF16)
    local_solve(u_ref, wide, inv_ref)
    put_strips(even_ref, odd_ref, u_ref)
    sum_out[...] = sum_ref[...] + sum_got[...]


def blocks_of(sub):
    own = sub - 2 * STRIP
    tall = 256
    return [None] + [slice(j * tall, (j + 1) * tall) for j in range(own // tall)]


def sides_of(ref, rows):
    sub = ref.shape[1]
    return jnp.concatenate([ref[rows, 0:STRIP], ref[rows, sub - STRIP :]], 1)


def inner_product(inner, o_ref, out_ref):
    own, sub = o_ref.shape
    rows = slice(STRIP, own - STRIP)
    for block in blocks_of(sub):
        if block is None:
            thru = lax.dot_general(inner, sides_of(o_ref, rows), NN, preferred_element_type=F32)
            out_ref[:, 0:STRIP] = thru[:, 0:STRIP]
            out_ref[:, sub - STRIP :] = thru[:, STRIP:]
            continue
        cols = slice(STRIP + block.start, STRIP + block.stop)
        part = lax.dot_general(inner, o_ref[rows, cols], NN, preferred_element_type=F32)
        out_ref[:, cols] = part + lax.dot_general(
            inner, o_ref[block, 2 * STRIP : sub - 2 * STRIP], NT, preferred_element_type=F32
        )


def outer_product(wide_ref, o_ref, thru_ref, deg, mass, out_ref):
    own, sub = o_ref.shape
    w = STRIP
    low, high = wide_ref[:, 0 : 2 * w].astype(BF16), wide_ref[:, sub - 2 * w :].astype(BF16)
    both = jnp.concatenate([low, high], 1)
    mine = jnp.concatenate([low[:, w:], high[:, 0:w]], 1)

    def rows(pick):
        return jnp.concatenate([pick(slice(0, w)), pick(slice(own - w, own))], 0)

    for block in blocks_of(sub):
        if block is None:
            part = lax.dot_general(
                mine, rows(lambda r: sides_of(o_ref, r)), NN, preferred_element_type=F32
            )
            for piece, start in ((part[:, 0:w], 0), (part[:, w:], sub - w)):
                cols = slice(start, start + w)
                piece = piece + thru_ref[:, cols]
                out_ref[:, cols] = wide_ref[:, cols] * deg(piece, cols) - piece
            continue
        cols = slice(w + block.start, w + block.stop)
        part = lax.dot_general(
            mine, rows(lambda r: o_ref[r, cols]), NN, preferred_element_type=F32
        )
        ends_of = jnp.concatenate([o_ref[block, 0 : 2 * w], o_ref[block, sub - 2 * w :]], 1)
        part = part + lax.dot_general(both, ends_of, NT, preferred_element_type=F32)
        part = part + thru_ref[:, cols]
        out_ref[:, cols] = wide_ref[:, cols] * (deg(part, cols) + mass[:, block]) - part


def fixed_rows(cvec, start, stop, sub):
    own = sub - 2 * STRIP
    lane = start + iota((1, stop - start), 1)
    return jnp.concatenate(
        [
            jnp.where(lane < STRIP, cvec, 0.0),
            jnp.where((lane >= STRIP) & (lane < STRIP + own), cvec, 0.0),
            jnp.where(lane >= STRIP + own, cvec, 0.0),
            jnp.ones(cvec.shape, F32),
            jnp.zeros((EXTRA - 4, stop - start), F32),
        ],
        0,
    )


def first_inner_kernel(u_ref, o_ref, cvec_ref, thru_ref):
    _, sub = u_ref.shape
    inner = slice(2 * STRIP, sub - 2 * STRIP)
    cvec = flat(cvec_ref)[:, STRIP : sub - 3 * STRIP]
    fixed = fixed_rows(cvec, inner.start, inner.stop, sub)
    value = jnp.concatenate([u_ref[:, inner], fixed], 0).astype(BF16)
    inner_product(value, o_ref, thru_ref)


def first_outer_kernel(
    n, u_ref, even_got, odd_got, halo_even, halo_odd, o_ref, thru_ref, cvec_ref, mass_ref, sum_ref,
    sum_got, s_ref, y_ref, deg_ref, even_ref, odd_ref, sum_out, wide_ref,
):
    rhs, sub = u_ref.shape
    left, right = take_sides(even_got[...], odd_got[...])
    vec_left, vec_right = take_sides(halo_even[rhs : rhs + 1, :], halo_odd[rhs : rhs + 1, :])
    wide_ref[0:rhs, :] = widen(u_ref, left, right, n)
    cvec = jnp.concatenate([vec_left, flat(cvec_ref), vec_right], 1)
    wide_ref[rhs:, :] = fixed_rows(cvec, 0, sub, sub)

    def degree(part, cols):
        row = part[rhs + 3 : rhs + 4, :]
        deg_ref[:, cols] = jnp.broadcast_to(row, (8, row.shape[1]))
        return row

    outer_product(wide_ref, o_ref, thru_ref, degree, flat(mass_ref), y_ref)
    s_ref[...] = wide_ref[0:rhs, STRIP : sub - STRIP]
    put_strips(even_ref, odd_ref, y_ref)
    sum_out[...] = sum_ref[...] + sum_got[...]


def add_coarse(value, vectors, coarse, first):
    for k in range(3):
        lane = first + k
        value = value + coarse[:, lane : lane + 1] * vectors[k : k + 1, :]
    return value


def solve_inner_kernel(y_ref, inv_ref, u_ref):
    sub = y_ref.shape[1]
    inner = slice(2 * STRIP, sub - 2 * STRIP)
    high = y_ref[:, inner].astype(BF16)
    tall = 256
    for j in range(sub // tall):
        cols = slice(j * tall, (j + 1) * tall)
        u_ref[:, cols] = jnp.dot(high, inv_ref[inner, cols], preferred_element_type=F32)


def solve_outer_kernel(
    n, y_ref, even_got, odd_got, sum_ref, sum_got, cinv_ref, inv_ref, half_ref,
    own_ref, u_ref, even_ref, odd_ref, sums_ref,
):
    rhs, sub = u_ref.shape
    w = STRIP
    first, last = ends(n)
    sums_ref[...] = sum_ref[...] + sum_got[...]
    coarse = coarse_columns(n, sums_ref[0:n, :], cinv_ref, 2)
    left, right = take_sides(even_got[...], odd_got[...])
    left = add_coarse(left[0:rhs], left[rhs : rhs + 3], coarse, 0)
    right = add_coarse(right[0:rhs], right[rhs : rhs + 3], coarse, 2)
    low, high = slice(0, 2 * w), slice(sub - 2 * w, sub)
    left = left + add_coarse(y_ref[0:rhs, low], y_ref[rhs : rhs + 3, low], coarse, 1)
    right = right + add_coarse(y_ref[0:rhs, high], y_ref[rhs : rhs + 3, high], coarse, 1)
    inner = slice(2 * w, sub - 2 * w)
    own_ref[:, 0:w] = left[:, w:]
    own_ref[:, w : sub - 3 * w] = add_coarse(
        y_ref[0:rhs, inner], y_ref[rhs : rhs + 3, inner], coarse, 1
    )
    own_ref[:, sub - 3 * w :] = right[:, 0:w]
    both = jnp.concatenate(
        [left[:, 0:w] * first, left[:, w:], right[:, 0:w], right[:, w:] * last], 1
    ).astype(BF16)
    tall = 256
    for j in range(sub // tall):
        cols = slice(j * tall, (j + 1) * tall)
        part = jnp.concatenate([inv_ref[low, cols], inv_ref[high, cols]], 0)
        part = jnp.dot(both, part, preferred_element_type=F32) + half_ref[0:rhs, cols]
        u_ref[:, cols] = add_coarse(part, half_ref[rhs : rhs + 3, cols], coarse, 1)
    put_strips(even_ref, odd_ref, u_ref)


def between_kernel(
    n, s_ref, y_ref, coarse_rows, even_got, odd_got, sums_ref, cinv_ref, cvec_ref, rhs_ref,
    z_ref, g_ref, part_ref,
):
    me, _ = place()
    rhs, own = s_ref.shape
    sub = own + 2 * STRIP
    slots = up(n, 8)
    coarse = coarse_columns(n, sums_ref[0:n, :], cinv_ref, 0)
    cvec = flat(cvec_ref)
    z = s_ref[...] + coarse[:, 0:1] * cvec
    z_ref[...] = z
    left, right = take_sides(even_got[rhs:, STRIP:], odd_got[rhs:, STRIP:])
    _, right = take_sides(even_got[rhs:, 0:STRIP], odd_got[rhs:, 0:STRIP])
    mine = coarse_rows[rhs:, STRIP : sub - STRIP]
    lefts = [left[1:2, :], left[2:3, :], None]
    rights = [None, right[0:1, :], right[1:2, :]]
    rows = []
    for k in range(3):
        head, body, tail = (
            mine[k : k + 1, 0:STRIP],
            mine[k : k + 1, STRIP : own - STRIP],
            mine[k : k + 1, own - STRIP :],
        )
        if lefts[k] is not None:
            head = head + lefts[k]
        if rights[k] is not None:
            tail = tail + rights[k]
        rows.append(jnp.concatenate([head, body, tail], 1))
    g = jnp.concatenate(rows + [jnp.zeros((5, own), F32)], 0)
    g_ref[...] = g
    part_ref[0:slots, :] = rows_of([(me, rowsum(y_ref[...] * cvec))], slots)
    shape = (slots, rhs)
    here = iota(shape, 0) == me
    inner = rowsum(g * cvec)
    total = jnp.zeros(shape, F32)
    for k in range(3):
        take = here & (iota(shape, 1) == k)
        total = total + jnp.where(take, jnp.broadcast_to(inner[k : k + 1, :], shape), 0.0)
    part_ref[slots : 2 * slots, :] = total
    a, b = rowsum(rhs_ref[...] * s_ref[...]), rowsum(z * y_ref[...])
    part_ref[2 * slots :, :] = rows_of([(0, a), (1, b)], 8)


def next_inner_kernel(u_ref, o_ref, rhs_ref, y_ref, g_ref, thru_ref, dots_ref):
    rhs, sub = u_ref.shape
    own = sub - 2 * STRIP
    value = u_ref[:, 2 * STRIP : sub - 2 * STRIP]
    inner_product(value.astype(BF16), o_ref, thru_ref)
    inner = slice(STRIP, own - STRIP)
    columns = [rowsum(value * rhs_ref[:, inner]), rowsum(value * y_ref[:, inner])]
    columns += [rowsum(value * g_ref[k : k + 1, inner]) for k in range(3)]
    lane = iota((rhs, LANES), 1)
    total = jnp.zeros((rhs, LANES), F32)
    for k, column in enumerate(columns):
        total = total + jnp.where(lane == k, jnp.broadcast_to(column, (rhs, LANES)), 0.0)
    dots_ref[...] = total


def next_outer_kernel(
    n, u_ref, even_got, odd_got, o_ref, thru_ref, dots_ref, deg_ref, mass_ref, rhs_ref, y_ref,
    g_ref, part_in, w_ref, q_ref, even_ref, odd_ref, part_ref, wide_ref, out_ref,
):
    me, even = place()
    rhs, sub = u_ref.shape
    own = sub - 2 * STRIP
    slots = up(n, 8)
    left, right = take_sides(even_got[...], odd_got[...])
    wide_ref[...] = widen(u_ref, left, right, n)
    outer_product(
        wide_ref, o_ref, thru_ref, lambda part, cols: deg_ref[0:1, cols], flat(mass_ref), out_ref
    )
    w_ref[...] = wide_ref[:, STRIP : sub - STRIP]
    q_ref[...] = out_ref[:, STRIP : sub - STRIP]
    e = rowsum(wide_ref[...] * out_ref[...])

    def edges_of(ref):
        return jnp.concatenate([ref[:, 0:STRIP], ref[:, own - STRIP :]], 1)

    w = jnp.concatenate(
        [wide_ref[:, STRIP : 2 * STRIP], wide_ref[:, sub - 2 * STRIP : sub - STRIP]], 1
    )
    g = edges_of(g_ref)
    c = dots_ref[:, 0:1] + rowsum(w * edges_of(rhs_ref))
    d = dots_ref[:, 1:2] + rowsum(w * edges_of(y_ref))
    cross = [
        (me - 1 + k, dots_ref[:, 2 + k : 3 + k] + rowsum(w * g[k : k + 1, :])) for k in range(3)
    ]
    part_ref[0 : 2 * slots, :] = part_in[0 : 2 * slots, :]
    part_ref[2 * slots : 3 * slots, :] = rows_of(cross, slots)
    part_ref[3 * slots :, :] = part_in[2 * slots :, :] + rows_of([(2, c), (3, d), (4, e)], 8)

    @pl.when(even)
    def _():
        even_ref[0:rhs, :] = out_ref[:, sub - STRIP :]
        odd_ref[...] = out_ref[:, 0:STRIP]

    @pl.when(jnp.logical_not(even))
    def _():
        even_ref[0:rhs, :] = out_ref[:, 0:STRIP]
        odd_ref[...] = out_ref[:, sub - STRIP :]

    even_ref[rhs:, :] = part_ref[...]


def finish_kernel(
    n, rhs_ref, z_ref, y_ref, w_ref, q_ref, g_ref, even_got, odd_got, first_ref, part_in, more_ref,
    cinv_ref, cvec_ref, x_hbm, r_hbm, x_ref, r_ref, sem,
):
    _, _ = place()
    rhs, own = rhs_ref.shape
    slots = up(n, 8)
    first = first_ref[0:n, :]
    part_ref = part_in[...] + more_ref[...]
    rho, cross = part_ref[0:n, :], part_ref[2 * slots : 2 * slots + n, :]
    gram = part_ref[slots : slots + n, :]
    sums = part_ref[3 * slots :, :]
    exact = dict(precision=HIGHEST, preferred_element_type=F32)

    def over(x):
        return jnp.sum(x, axis=0, keepdims=True)

    start = lax.dot_general(cinv_ref[...], first, TN, **exact)
    level = lax.dot_general(cinv_ref[...], rho, TN, **exact)
    shape = (n, n)
    band = jnp.zeros(shape, F32)
    for k in range(3):
        take = iota(shape, 1) == iota(shape, 0) + (k - 1)
        band = band + jnp.where(take, jnp.broadcast_to(gram[:, k : k + 1], shape), 0.0)
    bent = jnp.dot(band, level, **exact)

    a = sums[0:1, :] + over(start * first)
    b = sums[1:2, :]
    c = sums[2:3, :] + over(level * first)
    d = sums[3:4, :] + over(level * rho)
    e = sums[4:5, :] + over(level * (2.0 * cross + bent))
    alpha = a / b
    following = a - alpha * (c + b) + alpha * alpha * d
    beta = following / a
    between = b - alpha * d
    energy = (b - 2.0 * alpha * d + alpha * alpha * e) + 2.0 * beta * between + beta * beta * b
    step = following / energy
    near = jnp.transpose(jnp.broadcast_to(alpha + step * (1.0 + beta), (LANES, rhs)))[:, 0:1]
    far = jnp.transpose(jnp.broadcast_to(alpha * step, (LANES, rhs)))[:, 0:1]
    coarse = coarse_columns(n, rho, cinv_ref, 1) * far
    cvec = flat(cvec_ref)
    left, right = take_sides(even_got[0:rhs, :], odd_got[...])
    edge = {0: far * left, own - STRIP: far * right}
    tall = rhs // CHUNKS
    copies = []
    for i in range(CHUNKS):
        at = slice(i * tall, (i + 1) * tall)
        p, s, c = near[at], far[at], coarse[at]
        x_ref[at, :] = p * z_ref[at, :] - s * w_ref[at, :] - c[:, 1:2] * cvec
        r_ref[at, :] = add_coarse(
            rhs_ref[at, :] - p * y_ref[at, :] + s * q_ref[at, :], g_ref[...], c, 0
        )
        for start, value in edge.items():
            r_ref[at, start : start + STRIP] += value[at]
        for k, (source, target) in enumerate(((x_ref, x_hbm), (r_ref, r_hbm))):
            copy = pltpu.make_async_copy(source.at[at, :], target.at[at, :], sem.at[k, i])
            copy.start()
            copies.append(copy)
    for copy in copies:
        copy.wait()


def call(kernel, outs, scratch, limit, count, in_specs=None, out_space=None, flops=0):
    vmem = pl.BlockSpec(memory_space=pltpu.VMEM)
    out_spec = vmem if out_space is None else pl.BlockSpec(memory_space=out_space)
    return pl.pallas_call(
        kernel,
        out_shape=[jax.ShapeDtypeStruct(s, d) for s, d in outs],
        in_specs=in_specs if in_specs is not None else [vmem] * count,
        out_specs=[out_spec] * len(outs),
        scratch_shapes=scratch,
        compiler_params=pltpu.CompilerParams(vmem_limit_bytes=limit << 20),
        cost_estimate=pl.CostEstimate(flops=flops, bytes_accessed=0, transcendentals=0),
    )


def swap(pair):
    n = lax.axis_size("tile")
    got = []
    for start, payload in zip((0, 1), pair):
        links = []
        for i in range(start, n - 1, 2):
            links += [(i, i + 1), (i + 1, i)]
        got.append(lax.ppermute(payload, "tile", links))
    return got


def across(part, hop):
    n = lax.axis_size("tile")
    if hop >= n:
        return jnp.zeros_like(part)
    return lax.ppermute(part, "tile", [(i, i ^ hop) for i in range(n)])


def finish_sum(part, hop):
    n = lax.axis_size("tile")
    while 2 * hop < n:
        part = part + across(part, hop)
        hop *= 2
    return part, across(part, hop)


def shards(
    rhs, mass_diag, edge_heads, edge_tails, edge_weight, local_inverse, coarse_vec, coarse_inv
):
    n = lax.axis_size("tile")
    if n < 2 or n & (n - 1):
        raise ValueError("tile axis")
    rows, own = rhs.shape
    sub = local_inverse.shape[1]
    edges = edge_heads.shape[0]
    slots = up(n, 8)
    cvec, mass = coarse_vec.reshape(-1, LANES), mass_diag.reshape(-1, LANES)
    vmem = pl.BlockSpec(memory_space=pltpu.VMEM)
    smem = pl.BlockSpec(memory_space=pltpu.SMEM)
    bind = functools.partial

    side = ((rows + 8 + slots, STRIP), F32)
    few = ((slots, rows), F32)
    hbm = pl.BlockSpec(memory_space=pltpu.HBM)
    even, odd, part = call(
        begin_kernel,
        [side, side, few],
        [pltpu.VMEM(rhs.shape, F32), pltpu.VMEM(cvec.shape, F32), pltpu.SemaphoreType.DMA((2,))],
        4,
        2,
        in_specs=[hbm, hbm],
    )(rhs, cvec)
    halo = swap((even, odd))
    part = part + halo[0][rows + 8 :]

    at = (edge_tails >> 7) * own + (edge_heads - STRIP)
    shape = (edges // LANES, LANES)
    stiff, token = call(
        build_kernel,
        [((own, sub), BF16), ((8, LANES), F32)],
        [pltpu.VMEM(shape, F32), pltpu.SemaphoreType.DMA, pltpu.VMEM((edges, LANES), F32)]
        + [pltpu.VMEM((sub // LANES * own, LANES), F32)] * 2,
        34,
        4,
        in_specs=[smem, vmem, vmem, hbm],
        flops=10**10,
    )(at, at.reshape(shape), (edge_tails & 127).reshape(shape), edge_weight.reshape(shape))

    whole, owned = ((rows, sub), F32), ((rows, own), F32)
    strip = ((rows, 2 * STRIP), BF16)
    extra = ((rows + EXTRA, sub), F32)
    u, even, odd, part = call(
        first_solve_kernel, [whole, strip, strip, few], [], 12, 7, flops=10**9
    )(rhs, *halo, local_inverse, token, part, across(part, 2))
    got = swap((even, odd))
    (thru,) = call(first_inner_kernel, [extra], [], 8, 3, flops=2 * 10**9)(
        u, stiff, cvec
    )
    strips = ((rows + EXTRA, 2 * STRIP), BF16)
    s, y_part, degree, even, odd, part = call(
        bind(first_outer_kernel, n),
        [owned, extra, ((8, sub), F32), strips, strips, few],
        [pltpu.VMEM(*extra)],
        12,
        11,
        flops=10**9,
    )(u, *got, *halo, stiff, thru, cvec, mass, part, across(part, 4))
    got_y = swap((even, odd))
    (half,) = call(solve_inner_kernel, [extra], [], 8, 2, flops=10**9)(y_part, local_inverse)
    y, u, even, odd, sums = call(
        bind(solve_outer_kernel, n), [owned, whole, strip, strip, few], [], 12, 8, flops=10**8
    )(y_part, *got_y, *finish_sum(part, 8), coarse_inv, local_inverse, half)
    got = swap((even, odd))
    z, g, part = call(
        bind(between_kernel, n),
        [owned, ((8, own), F32), ((2 * slots + 8, rows), F32)],
        [],
        8,
        9,
        flops=10**9,
    )(s, y, y_part, *got_y, sums, coarse_inv, cvec, rhs)
    thru, dots = call(
        next_inner_kernel, [whole, ((rows, LANES), F32)], [], 8, 5, flops=2 * 10**9
    )(u, stiff, rhs, y, g)
    many = 3 * slots + 8
    w, q, even, odd, part = call(
        bind(next_outer_kernel, n),
        [owned, owned, ((rows + many, STRIP), F32), ((rows, STRIP), F32), ((many, rows), F32)],
        [pltpu.VMEM(*whole), pltpu.VMEM(*whole)],
        12,
        12,
        flops=10**9,
    )(u, *got, stiff, thru, dots, degree, mass, rhs, y, g, part)
    got = swap((even, odd))
    part, more = finish_sum(part + got[0][rows:], 2)
    return tuple(
        call(
            bind(finish_kernel, n),
            [owned, owned],
            [pltpu.VMEM(*owned)] * 2 + [pltpu.SemaphoreType.DMA((2, CHUNKS))],
            16,
            13,
            out_space=pltpu.HBM,
        )(rhs, z, y, w, q, g, *got, sums, part, more, coarse_inv, cvec)
    )


def solution(mesh):
    return jax.shard_map(
        shards,
        mesh=mesh,
        in_specs=(
            P("grp", "tile"),
            P("tile"),
            P("tile"),
            P("tile"),
            P("tile"),
            P("tile", None),
            P("tile"),
            P(),
        ),
        out_specs=(P("grp", "tile"), P("grp", "tile")),
        check_vma=False,
    )
```

```python
import functools

import jax
import jax.numpy as jnp
from jax import lax
from jax.experimental import pallas as pl
from jax.experimental.pallas import tpu as pltpu
from jax.sharding import PartitionSpec as P

STRIP = 128
LANES = 128
GROUP = 8
EXTRA = 16
CHUNKS = 4
F32 = jnp.float32
BF16 = jnp.bfloat16
NN = (((1,), (0,)), ((), ()))
NT = (((1,), (1,)), ((), ()))
TN = (((0,), (0,)), ((), ()))
HIGHEST = lax.Precision.HIGHEST


def up(value, unit):
    return -(-value // unit) * unit


def iota(shape, dim):
    return lax.broadcasted_iota(jnp.int32, shape, dim)


def place():
    me = lax.axis_index("tile").astype(jnp.int32)
    return me, lax.rem(me, jnp.int32(2)) == 0


def ends(n):
    me, _ = place()
    return (
        jnp.where(me > 0, 1.0, 0.0).astype(F32),
        jnp.where(me < n - 1, 1.0, 0.0).astype(F32),
    )


def put_sides(even_ref, odd_ref, left, right):
    _, even = place()

    @pl.when(even)
    def _():
        even_ref[...] = right
        odd_ref[...] = left

    @pl.when(jnp.logical_not(even))
    def _():
        even_ref[...] = left
        odd_ref[...] = right


def take_sides(even_got, odd_got):
    _, even = place()
    flag = jnp.where(even, 1.0, 0.0).astype(F32)
    a, b = even_got.astype(F32), odd_got.astype(F32)
    return jnp.where(flag > 0, b, a), jnp.where(flag > 0, a, b)


def flat(ref):
    return jnp.concatenate([ref[i : i + 1, :] for i in range(ref.shape[0])], 1)


def widen(own, got_left, got_right, n):
    first, last = ends(n)
    w = STRIP
    sub = own.shape[1]
    return jnp.concatenate(
        [
            (own[:, 0:w] + got_left[:, 0:w]) * first,
            own[:, w : 2 * w] + got_left[:, w:],
            own[:, 2 * w : sub - 2 * w],
            own[:, sub - 2 * w : sub - w] + got_right[:, 0:w],
            (own[:, sub - w :] + got_right[:, w:]) * last,
        ],
        1,
    )


def rows_of(columns, count):
    rhs = columns[0][1].shape[0]
    wide = up(count, LANES)
    lane = iota((rhs, wide), 1)
    total = jnp.zeros((rhs, wide), F32)
    for slot, column in columns:
        total = total + jnp.where(lane == slot, jnp.broadcast_to(column, (rhs, wide)), 0.0)
    return jnp.transpose(total)[0:count]


def rowsum(x):
    return jnp.sum(x, axis=1, keepdims=True)


def coarse_columns(n, sums, cinv_ref, reach):
    me, _ = place()
    shape = (n, LANES)
    lane = iota(shape, 1)
    pick = (iota(shape, 0) == me - reach + lane) & (lane <= 2 * reach)
    columns = jnp.dot(
        cinv_ref[...], jnp.where(pick, 1.0, 0.0), precision=HIGHEST, preferred_element_type=F32
    )
    return lax.dot_general(sums, columns, TN, precision=HIGHEST, preferred_element_type=F32)


def begin_kernel(rhs_hbm, cvec_hbm, even_ref, odd_ref, part_ref, rhs_ref, cvec_ref, sem):
    me, _ = place()
    _, own = rhs_ref.shape
    slots = part_ref.shape[0]
    copies = [
        pltpu.make_async_copy(rhs_hbm, rhs_ref, sem.at[0]),
        pltpu.make_async_copy(cvec_hbm, cvec_ref, sem.at[1]),
    ]
    for copy in copies:
        copy.start()
    for copy in copies:
        copy.wait()
    cvec = flat(cvec_ref)
    part = rows_of([(me, rowsum(rhs_ref[...] * cvec))], slots)
    part_ref[...] = part

    def side(start):
        pad = jnp.zeros((7, STRIP), F32)
        cols = slice(start, start + STRIP)
        return jnp.concatenate([rhs_ref[:, cols], cvec[:, cols], pad, part], 0)

    put_sides(even_ref, odd_ref, side(0), side(own - STRIP))


def build_kernel(rows_v, lane_v, weight_ref, o_ref, token, *scratch):
    token[...] = jnp.zeros(token.shape, F32)
    turned_ref, picked, sem, merged = scratch[:4]
    tables, lists = scratch[4:6], scratch[6:]
    own, sub = o_ref.shape
    edges = merged.shape[0]
    blocks = edges // LANES
    panels = sub // LANES
    height = panels * own
    chunk = up(-(-height // blocks), 8)
    group = len(lists) // len(tables)

    fill = up(blocks, LANES) - blocks
    turned = jnp.transpose(
        jnp.concatenate([rows_v[...], jnp.zeros((fill, LANES), jnp.int32)], 0)
    )
    turned_ref[...] = turned
    turns = LANES // len(lists)
    copies = []
    for i, target in enumerate(lists):
        picked[i] = turned_ref[pl.ds(i, turns, stride=len(lists)), :]
        copies.append(pltpu.make_async_copy(picked.at[i], target, sem.at[i]))
        copies[-1].start()
    weights = weight_ref[...].astype(F32)
    square = (LANES, LANES)
    down, across = iota(square, 0), iota(square, 1)
    same_group = (down // group) == (across // group)
    for k in range(blocks):
        equal = jnp.broadcast_to(turned[:, k : k + 1], square) == jnp.broadcast_to(
            rows_v[k : k + 1, :], square
        )
        equal = jnp.where(equal & same_group, 1.0, 0.0).astype(BF16)
        hit = down == jnp.broadcast_to(lane_v[k : k + 1, :], square)
        spread = jnp.where(hit, jnp.broadcast_to(weights[k : k + 1, :], square), 0.0)
        merged[k * LANES : (k + 1) * LANES, :] = lax.dot_general(
            equal, spread.astype(BF16), NT, preferred_element_type=F32
        )
        low = min(k * chunk, height)
        high = min(low + chunk, height)
        if high > low:
            blank = jnp.concatenate([spread[LANES - 8 :, :] * 0.0] * ((high - low) // 8), 0)
            for acc in tables:
                acc[low:high, :] = blank
    for copy in copies:
        copy.wait()

    def add(k, _):
        base = k * LANES
        for j in range(turns):
            for half, acc in enumerate(tables):
                first = half * group
                at = [lists[first + i][j, k] for i in range(group)]
                start = pl.multiple_of(base + j * len(lists) + first, group)
                new = merged[pl.ds(start, group), :]
                out = [acc[pl.ds(at[i], 1), :] + new[i : i + 1, :] for i in range(group)]
                for i in range(group):
                    acc[pl.ds(at[i], 1), :] = out[i]
        return 0

    lax.fori_loop(0, blocks, add, 0)

    tall = 256

    def narrow(i, _):
        for p in range(panels):
            rows = pl.ds(pl.multiple_of(p * own + i * tall, tall), tall)
            value = tables[0][rows, :] + tables[1][rows, :]
            o_ref[pl.ds(pl.multiple_of(i * tall, tall), tall), p * LANES : (p + 1) * LANES] = (
                value.astype(BF16)
            )
        return 0

    lax.fori_loop(0, own // tall, narrow, 0)


def local_solve(u_ref, wide, inv_ref):
    tall = 256
    for j in range(u_ref.shape[1] // tall):
        cols = slice(j * tall, (j + 1) * tall)
        u_ref[:, cols] = jnp.dot(wide, inv_ref[:, cols], preferred_element_type=F32)


def put_strips(even_ref, odd_ref, ref):
    width = even_ref.shape[1]
    sub = ref.shape[1]
    put_sides(
        even_ref, odd_ref, ref[:, 0:width].astype(BF16), ref[:, sub - width :].astype(BF16)
    )


def first_solve_kernel(
    rhs_ref, even_got, odd_got, inv_ref, token, sum_ref, sum_got, u_ref, even_ref, odd_ref, sum_out
):
    rhs = rhs_ref.shape[0]
    left, right = take_sides(even_got[0:rhs, :], odd_got[0:rhs, :])
    wide = jnp.concatenate([left, rhs_ref[...], right], 1).astype(BF16)
    local_solve(u_ref, wide, inv_ref)
    put_strips(even_ref, odd_ref, u_ref)
    sum_out[...] = sum_ref[...] + sum_got[...]


def blocks_of(sub):
    own = sub - 2 * STRIP
    tall = 256
    return [None] + [slice(j * tall, (j + 1) * tall) for j in range(own // tall)]


def sides_of(ref, rows):
    sub = ref.shape[1]
    return jnp.concatenate([ref[rows, 0:STRIP], ref[rows, sub - STRIP :]], 1)


def inner_product(inner, o_ref, out_ref):
    own, sub = o_ref.shape
    rows = slice(STRIP, own - STRIP)
    for block in blocks_of(sub):
        if block is None:
            thru = lax.dot_general(inner, sides_of(o_ref, rows), NN, preferred_element_type=F32)
            out_ref[:, 0:STRIP] = thru[:, 0:STRIP]
            out_ref[:, sub - STRIP :] = thru[:, STRIP:]
            continue
        cols = slice(STRIP + block.start, STRIP + block.stop)
        part = lax.dot_general(inner, o_ref[rows, cols], NN, preferred_element_type=F32)
        out_ref[:, cols] = part + lax.dot_general(
            inner, o_ref[block, 2 * STRIP : sub - 2 * STRIP], NT, preferred_element_type=F32
        )


def outer_product(wide_ref, o_ref, thru_ref, deg, mass, out_ref):
    own, sub = o_ref.shape
    w = STRIP
    low, high = wide_ref[:, 0 : 2 * w].astype(BF16), wide_ref[:, sub - 2 * w :].astype(BF16)
    both = jnp.concatenate([low, high], 1)
    mine = jnp.concatenate([low[:, w:], high[:, 0:w]], 1)

    def rows(pick):
        return jnp.concatenate([pick(slice(0, w)), pick(slice(own - w, own))], 0)

    for block in blocks_of(sub):
        if block is None:
            part = lax.dot_general(
                mine, rows(lambda r: sides_of(o_ref, r)), NN, preferred_element_type=F32
            )
            for piece, start in ((part[:, 0:w], 0), (part[:, w:], sub - w)):
                cols = slice(start, start + w)
                piece = piece + thru_ref[:, cols]
                out_ref[:, cols] = wide_ref[:, cols] * deg(piece, cols) - piece
            continue
        cols = slice(w + block.start, w + block.stop)
        part = lax.dot_general(
            mine, rows(lambda r: o_ref[r, cols]), NN, preferred_element_type=F32
        )
        ends_of = jnp.concatenate([o_ref[block, 0 : 2 * w], o_ref[block, sub - 2 * w :]], 1)
        part = part + lax.dot_general(both, ends_of, NT, preferred_element_type=F32)
        part = part + thru_ref[:, cols]
        out_ref[:, cols] = wide_ref[:, cols] * (deg(part, cols) + mass[:, block]) - part


def fixed_rows(cvec, start, stop, sub):
    own = sub - 2 * STRIP
    lane = start + iota((1, stop - start), 1)
    return jnp.concatenate(
        [
            jnp.where(lane < STRIP, cvec, 0.0),
            jnp.where((lane >= STRIP) & (lane < STRIP + own), cvec, 0.0),
            jnp.where(lane >= STRIP + own, cvec, 0.0),
            jnp.ones(cvec.shape, F32),
            jnp.zeros((EXTRA - 4, stop - start), F32),
        ],
        0,
    )


def first_inner_kernel(u_ref, o_ref, cvec_ref, thru_ref):
    _, sub = u_ref.shape
    inner = slice(2 * STRIP, sub - 2 * STRIP)
    cvec = flat(cvec_ref)[:, STRIP : sub - 3 * STRIP]
    fixed = fixed_rows(cvec, inner.start, inner.stop, sub)
    value = jnp.concatenate([u_ref[:, inner], fixed], 0).astype(BF16)
    inner_product(value, o_ref, thru_ref)


def first_outer_kernel(
    n, u_ref, even_got, odd_got, halo_even, halo_odd, o_ref, thru_ref, cvec_ref, mass_ref, sum_ref,
    sum_got, s_ref, y_ref, deg_ref, even_ref, odd_ref, sum_out, wide_ref,
):
    rhs, sub = u_ref.shape
    left, right = take_sides(even_got[...], odd_got[...])
    vec_left, vec_right = take_sides(halo_even[rhs : rhs + 1, :], halo_odd[rhs : rhs + 1, :])
    wide_ref[0:rhs, :] = widen(u_ref, left, right, n)
    cvec = jnp.concatenate([vec_left, flat(cvec_ref), vec_right], 1)
    wide_ref[rhs:, :] = fixed_rows(cvec, 0, sub, sub)

    def degree(part, cols):
        row = part[rhs + 3 : rhs + 4, :]
        deg_ref[:, cols] = jnp.broadcast_to(row, (8, row.shape[1]))
        return row

    outer_product(wide_ref, o_ref, thru_ref, degree, flat(mass_ref), y_ref)
    s_ref[...] = wide_ref[0:rhs, STRIP : sub - STRIP]
    put_strips(even_ref, odd_ref, y_ref)
    sum_out[...] = sum_ref[...] + sum_got[...]


def add_coarse(value, vectors, coarse, first):
    for k in range(3):
        lane = first + k
        value = value + coarse[:, lane : lane + 1] * vectors[k : k + 1, :]
    return value


def solve_inner_kernel(y_ref, inv_ref, u_ref):
    sub = y_ref.shape[1]
    inner = slice(2 * STRIP, sub - 2 * STRIP)
    high = y_ref[:, inner].astype(BF16)
    tall = 256
    for j in range(sub // tall):
        cols = slice(j * tall, (j + 1) * tall)
        u_ref[:, cols] = jnp.dot(high, inv_ref[inner, cols], preferred_element_type=F32)


def solve_outer_kernel(
    n, y_ref, even_got, odd_got, sum_ref, sum_got, cinv_ref, inv_ref, half_ref,
    own_ref, u_ref, even_ref, odd_ref, sums_ref,
):
    rhs, sub = u_ref.shape
    w = STRIP
    first, last = ends(n)
    sums_ref[...] = sum_ref[...] + sum_got[...]
    coarse = coarse_columns(n, sums_ref[0:n, :], cinv_ref, 2)
    left, right = take_sides(even_got[...], odd_got[...])
    left = add_coarse(left[0:rhs], left[rhs : rhs + 3], coarse, 0)
    right = add_coarse(right[0:rhs], right[rhs : rhs + 3], coarse, 2)
    low, high = slice(0, 2 * w), slice(sub - 2 * w, sub)
    left = left + add_coarse(y_ref[0:rhs, low], y_ref[rhs : rhs + 3, low], coarse, 1)
    right = right + add_coarse(y_ref[0:rhs, high], y_ref[rhs : rhs + 3, high], coarse, 1)
    inner = slice(2 * w, sub - 2 * w)
    own_ref[:, 0:w] = left[:, w:]
    own_ref[:, w : sub - 3 * w] = add_coarse(
        y_ref[0:rhs, inner], y_ref[rhs : rhs + 3, inner], coarse, 1
    )
    own_ref[:, sub - 3 * w :] = right[:, 0:w]
    both = jnp.concatenate(
        [left[:, 0:w] * first, left[:, w:], right[:, 0:w], right[:, w:] * last], 1
    ).astype(BF16)
    tall = 256
    for j in range(sub // tall):
        cols = slice(j * tall, (j + 1) * tall)
        part = jnp.concatenate([inv_ref[low, cols], inv_ref[high, cols]], 0)
        part = jnp.dot(both, part, preferred_element_type=F32) + half_ref[0:rhs, cols]
        u_ref[:, cols] = add_coarse(part, half_ref[rhs : rhs + 3, cols], coarse, 1)
    put_strips(even_ref, odd_ref, u_ref)


def between_kernel(
    n, s_ref, y_ref, coarse_rows, even_got, odd_got, sums_ref, cinv_ref, cvec_ref, rhs_ref,
    z_ref, g_ref, part_ref,
):
    me, _ = place()
    rhs, own = s_ref.shape
    sub = own + 2 * STRIP
    slots = up(n, 8)
    coarse = coarse_columns(n, sums_ref[0:n, :], cinv_ref, 0)
    cvec = flat(cvec_ref)
    z = s_ref[...] + coarse[:, 0:1] * cvec
    z_ref[...] = z
    left, right = take_sides(even_got[rhs:, STRIP:], odd_got[rhs:, STRIP:])
    _, right = take_sides(even_got[rhs:, 0:STRIP], odd_got[rhs:, 0:STRIP])
    mine = coarse_rows[rhs:, STRIP : sub - STRIP]
    lefts = [left[1:2, :], left[2:3, :], None]
    rights = [None, right[0:1, :], right[1:2, :]]
    rows = []
    for k in range(3):
        head, body, tail = (
            mine[k : k + 1, 0:STRIP],
            mine[k : k + 1, STRIP : own - STRIP],
            mine[k : k + 1, own - STRIP :],
        )
        if lefts[k] is not None:
            head = head + lefts[k]
        if rights[k] is not None:
            tail = tail + rights[k]
        rows.append(jnp.concatenate([head, body, tail], 1))
    g = jnp.concatenate(rows + [jnp.zeros((5, own), F32)], 0)
    g_ref[...] = g
    part_ref[0:slots, :] = rows_of([(me, rowsum(y_ref[...] * cvec))], slots)
    shape = (slots, rhs)
    here = iota(shape, 0) == me
    inner = rowsum(g * cvec)
    total = jnp.zeros(shape, F32)
    for k in range(3):
        take = here & (iota(shape, 1) == k)
        total = total + jnp.where(take, jnp.broadcast_to(inner[k : k + 1, :], shape), 0.0)
    part_ref[slots : 2 * slots, :] = total
    a, b = rowsum(rhs_ref[...] * s_ref[...]), rowsum(z * y_ref[...])
    part_ref[2 * slots :, :] = rows_of([(0, a), (1, b)], 8)


def next_inner_kernel(u_ref, o_ref, rhs_ref, y_ref, g_ref, thru_ref, dots_ref):
    rhs, sub = u_ref.shape
    own = sub - 2 * STRIP
    value = u_ref[:, 2 * STRIP : sub - 2 * STRIP]
    inner_product(value.astype(BF16), o_ref, thru_ref)
    inner = slice(STRIP, own - STRIP)
    columns = [rowsum(value * rhs_ref[:, inner]), rowsum(value * y_ref[:, inner])]
    columns += [rowsum(value * g_ref[k : k + 1, inner]) for k in range(3)]
    lane = iota((rhs, LANES), 1)
    total = jnp.zeros((rhs, LANES), F32)
    for k, column in enumerate(columns):
        total = total + jnp.where(lane == k, jnp.broadcast_to(column, (rhs, LANES)), 0.0)
    dots_ref[...] = total


def next_outer_kernel(
    n, u_ref, even_got, odd_got, o_ref, thru_ref, dots_ref, deg_ref, mass_ref, rhs_ref, y_ref,
    g_ref, part_in, w_ref, q_ref, even_ref, odd_ref, part_ref, wide_ref, out_ref,
):
    me, even = place()
    rhs, sub = u_ref.shape
    own = sub - 2 * STRIP
    slots = up(n, 8)
    left, right = take_sides(even_got[...], odd_got[...])
    wide_ref[...] = widen(u_ref, left, right, n)
    outer_product(
        wide_ref, o_ref, thru_ref, lambda part, cols: deg_ref[0:1, cols], flat(mass_ref), out_ref
    )
    w_ref[...] = wide_ref[:, STRIP : sub - STRIP]
    q_ref[...] = out_ref[:, STRIP : sub - STRIP]
    e = rowsum(wide_ref[...] * out_ref[...])

    def edges_of(ref):
        return jnp.concatenate([ref[:, 0:STRIP], ref[:, own - STRIP :]], 1)

    w = jnp.concatenate(
        [wide_ref[:, STRIP : 2 * STRIP], wide_ref[:, sub - 2 * STRIP : sub - STRIP]], 1
    )
    g = edges_of(g_ref)
    c = dots_ref[:, 0:1] + rowsum(w * edges_of(rhs_ref))
    d = dots_ref[:, 1:2] + rowsum(w * edges_of(y_ref))
    cross = [
        (me - 1 + k, dots_ref[:, 2 + k : 3 + k] + rowsum(w * g[k : k + 1, :])) for k in range(3)
    ]
    part_ref[0 : 2 * slots, :] = part_in[0 : 2 * slots, :]
    part_ref[2 * slots : 3 * slots, :] = rows_of(cross, slots)
    part_ref[3 * slots :, :] = part_in[2 * slots :, :] + rows_of([(2, c), (3, d), (4, e)], 8)

    @pl.when(even)
    def _():
        even_ref[0:rhs, :] = out_ref[:, sub - STRIP :]
        odd_ref[...] = out_ref[:, 0:STRIP]

    @pl.when(jnp.logical_not(even))
    def _():
        even_ref[0:rhs, :] = out_ref[:, 0:STRIP]
        odd_ref[...] = out_ref[:, sub - STRIP :]

    even_ref[rhs:, :] = part_ref[...]


def finish_kernel(
    n, rhs_ref, z_ref, y_ref, w_ref, q_ref, g_ref, even_got, odd_got, first_ref, part_in, more_ref,
    cinv_ref, cvec_ref, x_hbm, r_hbm, x_ref, r_ref, sem,
):
    _, _ = place()
    rhs, own = rhs_ref.shape
    slots = up(n, 8)
    first = first_ref[0:n, :]
    part_ref = part_in[...] + more_ref[...]
    rho, cross = part_ref[0:n, :], part_ref[2 * slots : 2 * slots + n, :]
    gram = part_ref[slots : slots + n, :]
    sums = part_ref[3 * slots :, :]
    exact = dict(precision=HIGHEST, preferred_element_type=F32)

    def over(x):
        return jnp.sum(x, axis=0, keepdims=True)

    start = lax.dot_general(cinv_ref[...], first, TN, **exact)
    level = lax.dot_general(cinv_ref[...], rho, TN, **exact)
    shape = (n, n)
    band = jnp.zeros(shape, F32)
    for k in range(3):
        take = iota(shape, 1) == iota(shape, 0) + (k - 1)
        band = band + jnp.where(take, jnp.broadcast_to(gram[:, k : k + 1], shape), 0.0)
    bent = jnp.dot(band, level, **exact)

    a = sums[0:1, :] + over(start * first)
    b = sums[1:2, :]
    c = sums[2:3, :] + over(level * first)
    d = sums[3:4, :] + over(level * rho)
    e = sums[4:5, :] + over(level * (2.0 * cross + bent))
    alpha = a / b
    following = a - alpha * (c + b) + alpha * alpha * d
    beta = following / a
    between = b - alpha * d
    energy = (b - 2.0 * alpha * d + alpha * alpha * e) + 2.0 * beta * between + beta * beta * b
    step = following / energy
    near = jnp.transpose(jnp.broadcast_to(alpha + step * (1.0 + beta), (LANES, rhs)))[:, 0:1]
    far = jnp.transpose(jnp.broadcast_to(alpha * step, (LANES, rhs)))[:, 0:1]
    coarse = coarse_columns(n, rho, cinv_ref, 1) * far
    cvec = flat(cvec_ref)
    left, right = take_sides(even_got[0:rhs, :], odd_got[...])
    edge = {0: far * left, own - STRIP: far * right}
    tall = rhs // CHUNKS
    copies = []
    for i in range(CHUNKS):
        at = slice(i * tall, (i + 1) * tall)
        p, s, c = near[at], far[at], coarse[at]
        x_ref[at, :] = p * z_ref[at, :] - s * w_ref[at, :] - c[:, 1:2] * cvec
        r_ref[at, :] = add_coarse(
            rhs_ref[at, :] - p * y_ref[at, :] + s * q_ref[at, :], g_ref[...], c, 0
        )
        for start, value in edge.items():
            r_ref[at, start : start + STRIP] += value[at]
        for k, (source, target) in enumerate(((x_ref, x_hbm), (r_ref, r_hbm))):
            copy = pltpu.make_async_copy(source.at[at, :], target.at[at, :], sem.at[k, i])
            copy.start()
            copies.append(copy)
    for copy in copies:
        copy.wait()


def call(kernel, outs, scratch, limit, count, in_specs=None, out_space=None, flops=0):
    vmem = pl.BlockSpec(memory_space=pltpu.VMEM)
    out_spec = vmem if out_space is None else pl.BlockSpec(memory_space=out_space)
    return pl.pallas_call(
        kernel,
        out_shape=[jax.ShapeDtypeStruct(s, d) for s, d in outs],
        in_specs=in_specs if in_specs is not None else [vmem] * count,
        out_specs=[out_spec] * len(outs),
        scratch_shapes=scratch,
        compiler_params=pltpu.CompilerParams(vmem_limit_bytes=limit << 20),
        cost_estimate=pl.CostEstimate(flops=flops, bytes_accessed=0, transcendentals=0),
    )


def swap(pair):
    n = lax.axis_size("tile")
    got = []
    for start, payload in zip((0, 1), pair):
        links = []
        for i in range(start, n - 1, 2):
            links += [(i, i + 1), (i + 1, i)]
        got.append(lax.ppermute(payload, "tile", links))
    return got


def across(part, hop):
    n = lax.axis_size("tile")
    if hop >= n:
        return jnp.zeros_like(part)
    return lax.ppermute(part, "tile", [(i, i ^ hop) for i in range(n)])


def finish_sum(part, hop):
    n = lax.axis_size("tile")
    while 2 * hop < n:
        part = part + across(part, hop)
        hop *= 2
    return part, across(part, hop)


def shards(
    rhs, mass_diag, edge_heads, edge_tails, edge_weight, local_inverse, coarse_vec, coarse_inv
):
    n = lax.axis_size("tile")
    if n < 2 or n & (n - 1):
        raise ValueError("tile axis")
    rows, own = rhs.shape
    sub = local_inverse.shape[1]
    edges = edge_heads.shape[0]
    slots = up(n, 8)
    cvec, mass = coarse_vec.reshape(-1, LANES), mass_diag.reshape(-1, LANES)
    vmem = pl.BlockSpec(memory_space=pltpu.VMEM)
    bind = functools.partial

    side = ((rows + 8 + slots, STRIP), F32)
    few = ((slots, rows), F32)
    hbm = pl.BlockSpec(memory_space=pltpu.HBM)
    even, odd, part = call(
        begin_kernel,
        [side, side, few],
        [pltpu.VMEM(rhs.shape, F32), pltpu.VMEM(cvec.shape, F32), pltpu.SemaphoreType.DMA((2,))],
        4,
        2,
        in_specs=[hbm, hbm],
    )(rhs, cvec)
    halo = swap((even, odd))
    part = part + halo[0][rows + 8 :]

    at = (edge_tails >> 7) * own + (edge_heads - STRIP)
    shape = (edges // LANES, LANES)
    weight = jnp.where(edge_tails >= 0, edge_weight, 0.0).astype(BF16)
    lists = 2 * GROUP
    stiff, token = call(
        build_kernel,
        [((own, sub), BF16), ((8, LANES), F32)],
        [
            pltpu.VMEM((LANES, LANES), jnp.int32),
            pltpu.VMEM((lists, LANES // lists, LANES), jnp.int32),
            pltpu.SemaphoreType.DMA((lists,)),
            pltpu.VMEM((edges, LANES), F32),
        ]
        + [pltpu.VMEM((sub // LANES * own, LANES), F32)] * 2
        + [pltpu.SMEM((LANES // lists, LANES), jnp.int32)] * lists,
        34,
        3,
        flops=10**10,
    )(at.reshape(shape), (edge_tails & 127).reshape(shape), weight.reshape(shape))

    whole, owned = ((rows, sub), F32), ((rows, own), F32)
    strip = ((rows, 2 * STRIP), BF16)
    extra = ((rows + EXTRA, sub), F32)
    u, even, odd, part = call(
        first_solve_kernel, [whole, strip, strip, few], [], 12, 7, flops=10**9
    )(rhs, *halo, local_inverse, token, part, across(part, 2))
    got = swap((even, odd))
    (thru,) = call(first_inner_kernel, [extra], [], 8, 3, flops=2 * 10**9)(
        u, stiff, cvec
    )
    strips = ((rows + EXTRA, 2 * STRIP), BF16)
    s, y_part, degree, even, odd, part = call(
        bind(first_outer_kernel, n),
        [owned, extra, ((8, sub), F32), strips, strips, few],
        [pltpu.VMEM(*extra)],
        12,
        11,
        flops=10**9,
    )(u, *got, *halo, stiff, thru, cvec, mass, part, across(part, 4))
    got_y = swap((even, odd))
    (half,) = call(solve_inner_kernel, [extra], [], 8, 2, flops=10**9)(y_part, local_inverse)
    y, u, even, odd, sums = call(
        bind(solve_outer_kernel, n), [owned, whole, strip, strip, few], [], 12, 8, flops=10**8
    )(y_part, *got_y, *finish_sum(part, 8), coarse_inv, local_inverse, half)
    got = swap((even, odd))
    z, g, part = call(
        bind(between_kernel, n),
        [owned, ((8, own), F32), ((2 * slots + 8, rows), F32)],
        [],
        8,
        9,
        flops=10**9,
    )(s, y, y_part, *got_y, sums, coarse_inv, cvec, rhs)
    thru, dots = call(
        next_inner_kernel, [whole, ((rows, LANES), F32)], [], 8, 5, flops=2 * 10**9
    )(u, stiff, rhs, y, g)
    many = 3 * slots + 8
    w, q, even, odd, part = call(
        bind(next_outer_kernel, n),
        [owned, owned, ((rows + many, STRIP), F32), ((rows, STRIP), F32), ((many, rows), F32)],
        [pltpu.VMEM(*whole), pltpu.VMEM(*whole)],
        12,
        12,
        flops=10**9,
    )(u, *got, stiff, thru, dots, degree, mass, rhs, y, g, part)
    got = swap((even, odd))
    part, more = finish_sum(part + got[0][rows:], 2)
    return tuple(
        call(
            bind(finish_kernel, n),
            [owned, owned],
            [pltpu.VMEM(*owned)] * 2 + [pltpu.SemaphoreType.DMA((2, CHUNKS))],
            16,
            13,
            out_space=pltpu.HBM,
        )(rhs, z, y, w, q, g, *got, sums, part, more, coarse_inv, cvec)
    )


def solution(mesh):
    return jax.shard_map(
        shards,
        mesh=mesh,
        in_specs=(
            P("grp", "tile"),
            P("tile"),
            P("tile"),
            P("tile"),
            P("tile"),
            P("tile", None),
            P("tile"),
            P(),
        ),
        out_specs=(P("grp", "tile"), P("grp", "tile")),
        check_vma=False,
    )
```
